32 devices in a mesh: group: 2 (over y), frame: 8 (over z, x), row: 2 (over core).
Axes of the slice: x: 2, y: 2, z: 4, core: 2. Of those that a mesh axis runs over, the one named last changes fastest.
Arguments:
- latents: bfloat16 [16, 8, 32, 1120], P(('group', 'frame'), 'row'), parts along dimension 0, may hold values from -24 to 24
- spatial_weights: bfloat16 [4, 10, 112, 112], replicated, may hold values from -0.5 to 0.5
- causal_weights: bfloat16 [4, 10, 112, 112], replicated, may hold values from -0.5 to 0.5
Outputs:
- updated_latents: bfloat16 [16, 8, 32, 1120], P(('group', 'frame'), None, None, 'row'), parts along dimension 0
The draws below stay inside these ranges and needn't reach their ends.
There are 2 independent parts, one for each index of `group`. The reference program is written for one: setup_inputs(seed, part) draws one part's arguments, and reference() takes and returns one part's arrays. A program takes and returns all parts, laid end to end along the dimension named above; an argument that names none is the same for every part. Nothing has to cross between parts.
All inputs are finite; a program needn't handle non-finite values.
Results may differ from the reference program's by a relative error of at most 0.0047.
The reference program's roundings to bfloat16 on the way count: a program that leaves them out, or rounds other values in their place, can miss the bound.
Values may be sent and summed in bfloat16 or wider, within the bound.
No kernel may reach another device: no remote copies, remote signals or barrier semaphores. Data moves between devices by JAX's collectives and lax.ppermute only.
A program may use at most 64 MiB of HBM per device.

```python
import jax
import jax.numpy as jnp
from jax import lax

HEADS = 10
HEAD_DIM = 112
WIDTH = 1120
COLS = 32
BAND_ROWS = 4
ROWS = 8
FRAMES = 8
N_ROW = 2


def draw_latents(key, part):
    keys = jax.random.split(jax.random.fold_in(key, 7001), 4)
    band_count = ROWS // BAND_ROWS
    ranks = 3
    frame_ids = jnp.arange(FRAMES, dtype=jnp.int32)
    fresh = jax.random.randint(keys[0], (FRAMES,), 0, 10) < 3
    fresh = jnp.logical_or(fresh, frame_ids == 0).astype(jnp.int32)
    segment = (jnp.cumsum(fresh) - 1).astype(jnp.int32)
    directions = jnp.clip(jax.random.normal(keys[1], (FRAMES, band_count, ranks, WIDTH), jnp.float32), -3.0, 3.0)
    picked = jnp.take(directions, segment, axis=0)
    weights_tok = jnp.clip(jax.random.normal(keys[2], (FRAMES, band_count, BAND_ROWS, COLS, ranks), jnp.float32), -3.0, 3.0)
    noise = jnp.clip(jax.random.normal(keys[3], (FRAMES, ROWS, COLS, WIDTH), jnp.float32), -4.0, 4.0)
    amplitude = 0.6
    structure = jnp.einsum('fbrcj,fbjw->fbrcw', weights_tok, picked).reshape(FRAMES, ROWS, COLS, WIDTH)
    return jnp.clip(noise + amplitude * structure, -24.0, 24.0).astype(jnp.bfloat16)


def centred(key, shape, width, reach, kind=jnp.bfloat16):
    entries = width * jax.random.normal(key, shape, jnp.float32)
    return jnp.clip(entries, min=-reach, max=reach).astype(kind)


def setup_inputs(seed: int = 0, part: int = 0) -> dict:
    key_of = jax.random.split(jax.random.key(seed), 4)
    part_splits = jax.random.split(jax.random.fold_in(key_of[3], part), 4)
    return {
        "latents": draw_latents(jax.random.fold_in(jax.random.fold_in(key_of[3], part), 71), part),
        "spatial_weights": centred(key_of[1], (4, HEADS, HEAD_DIM, HEAD_DIM), HEAD_DIM ** -0.5, 0.5),
        "causal_weights": centred(key_of[2], (4, HEADS, HEAD_DIM, HEAD_DIM), HEAD_DIM ** -0.5, 0.5),
    }


def project(frame_block, weights):
    flat_rows = frame_block.reshape(-1, HEADS * HEAD_DIM).astype(jnp.float32)
    normed = (flat_rows * lax.rsqrt(lax.optimization_barrier(jnp.mean(flat_rows * flat_rows, axis=-1, keepdims=True)) + 1e-06)).astype(jnp.bfloat16)
    normed = normed.reshape(-1, HEADS, HEAD_DIM).astype(jnp.float32)
    mapped = jnp.einsum('thd,khde->kthe', normed, weights.astype(jnp.float32))
    queries = jax.nn.relu(mapped[0]).astype(jnp.bfloat16)
    key_rows = jax.nn.relu(mapped[1]).astype(jnp.bfloat16)
    value_rows = mapped[2].astype(jnp.bfloat16)
    gating = jax.nn.sigmoid(mapped[3])
    return (queries, key_rows, value_rows, gating)

def band_states(frame_block, weights):
    _, key_rows, value_rows, _ = project(frame_block, weights)
    key_bands = key_rows.reshape(N_ROW, BAND_ROWS * COLS, HEADS, HEAD_DIM).astype(jnp.float32)
    value_bands = value_rows.reshape(N_ROW, BAND_ROWS * COLS, HEADS, HEAD_DIM).astype(jnp.float32)
    return jnp.einsum('bthd,bthe->bhde', key_bands, value_bands)

def finish_frame(frame_block, weights, states):
    queries, _, _, gating = project(frame_block, weights)
    query_bands = queries.reshape(N_ROW, BAND_ROWS * COLS, HEADS, HEAD_DIM).astype(jnp.float32)
    attended = jnp.einsum('bthd,bhde->bthe', query_bands, states, precision=lax.Precision.HIGHEST)
    attended = attended.reshape(-1, HEADS, HEAD_DIM)
    inv_rms = lax.rsqrt(lax.optimization_barrier(jnp.mean(attended * attended, axis=-1, keepdims=True)) + 1e-05)
    branch = (gating * attended * inv_rms).reshape(frame_block.shape)
    return (frame_block.astype(jnp.float32) + branch).astype(jnp.bfloat16)

def reference(latents, spatial_weights, causal_weights):
    spatial_bands = lax.map(lambda frame_block: band_states(frame_block, spatial_weights), latents)
    whole_frame = jnp.broadcast_to(lax.optimization_barrier(jnp.sum(spatial_bands, axis=1, keepdims=True)), spatial_bands.shape)
    mixed_video = lax.map(lambda pair: finish_frame(pair[0], spatial_weights, pair[1]), (latents, whole_frame))
    causal_bands = lax.map(lambda frame_block: band_states(frame_block, causal_weights), mixed_video)
    causal_whole = lax.optimization_barrier(jnp.sum(causal_bands, axis=1, keepdims=True))
    prefix = jnp.broadcast_to(jnp.cumsum(causal_whole, axis=0), causal_bands.shape)
    return lax.map(lambda pair: finish_frame(pair[0], causal_weights, pair[1]), (mixed_video, prefix))
```

```python
import functools

import jax
import jax.numpy as jnp
from jax import lax
from jax.experimental import pallas as pl
from jax.experimental.pallas import tpu as pltpu
from jax.sharding import PartitionSpec as P

LANES = 128
F32 = jnp.float32
BF16 = jnp.bfloat16
VMEM = pl.BlockSpec(memory_space=pltpu.VMEM)
SMEM = pl.BlockSpec(memory_space=pltpu.SMEM)


def call(kernel, name, out_shape, operands, in_specs, scratch=(), flops=0, limit=24 << 20):
    n_bytes = sum(o.size * o.dtype.itemsize for o in operands)
    n_bytes += sum(o.size * o.dtype.itemsize for o in out_shape)
    return pl.pallas_call(
        kernel,
        name=name,
        out_shape=tuple(out_shape),
        in_specs=in_specs,
        out_specs=tuple(VMEM for _ in out_shape),
        scratch_shapes=list(scratch),
        compiler_params=pltpu.CompilerParams(vmem_limit_bytes=limit),
        cost_estimate=pl.CostEstimate(flops=flops, bytes_accessed=n_bytes, transcendentals=0),
    )(*operands)


def pack_kernel(heads, row_ref, *refs):
    half = len(refs) // 2
    first = row_ref[0] * heads
    for w_ref, out_ref in zip(refs[:half], refs[half:]):
        maps, dim = w_ref.shape[0], w_ref.shape[2]
        out_ref[...] = jnp.zeros_like(out_ref)
        for h in range(heads):
            for m in range(maps):
                out_ref[h, :dim, m * LANES : m * LANES + dim] = w_ref[m, first + h]


def spatial_kernel(heads, dim, n_row, row_ref, own_ref, other_ref, w_ref, mixed_ref, part_ref, x_ref, inv_ref):
    band, width = own_ref.shape
    row = row_ref[0]
    x_ref[...] = jnp.zeros_like(x_ref)
    for src, place in ((own_ref, row), (other_ref, n_row - 1 - row)):
        at = pl.ds(pl.multiple_of(place * band, band), band)
        full = src[...].astype(F32)
        inv = lax.rsqrt(jnp.sum(full * full, axis=-1, keepdims=True) / width + 1e-06)
        inv_ref[at, :] = jnp.broadcast_to(inv, (band, LANES))
        for r in range(n_row):

            @pl.when(row == r)
            def _():
                for h in range(heads):
                    lo = (r * heads + h) * dim
                    x_ref[h, at, :dim] = src[:, lo : lo + dim]

    inv = inv_ref[...]
    part = jnp.zeros(part_ref.shape, F32)
    for h in range(heads):
        x = x_ref[h].astype(F32)
        u = (x * inv).astype(BF16)
        mapped = jnp.dot(u, w_ref[h], preferred_element_type=F32)
        q = jnp.maximum(mapped[:, :LANES], 0.0).astype(BF16)
        k = jnp.maximum(mapped[:, LANES : 2 * LANES], 0.0).astype(BF16)
        v = mapped[:, 2 * LANES : 3 * LANES].astype(BF16)
        gate = jax.nn.sigmoid(mapped[:, 3 * LANES :])
        state = lax.dot_general(k, v, (((0,), (0,)), ((), ())), preferred_element_type=F32)
        mixed = finish(x, gate, attend(q, state), dim)
        mixed_ref[h] = mixed
        wide = mixed.astype(F32)
        part = part + wide * wide
    part_ref[...] = part


def attend(q, state):
    high = state.astype(BF16)
    low = (state - high.astype(F32)).astype(BF16)
    return jnp.dot(
        jnp.concatenate([q, q], axis=1),
        jnp.concatenate([high, low], axis=0),
        preferred_element_type=F32,
    )


def finish(x, gate, attended, dim):
    inv_rms = lax.rsqrt(jnp.sum(attended * attended, axis=-1, keepdims=True) / dim + 1e-05)
    return (x + gate * attended * inv_rms).astype(BF16)


def state_kernel(heads, dim, width, mixed_ref, part_ref, part_other_ref, w_ref, normed_ref, state_ref, sent_ref):
    total = jnp.sum(part_ref[...] + part_other_ref[...], axis=-1, keepdims=True)
    inv = lax.rsqrt(total / width + 1e-06)
    for h in range(heads):
        u = (mixed_ref[h].astype(F32) * inv).astype(BF16)
        normed_ref[h] = u
        mapped = jnp.dot(u, w_ref[h, :, LANES : 3 * LANES], preferred_element_type=F32)
        k = jnp.maximum(mapped[:, :LANES], 0.0).astype(BF16)
        v = mapped[:, LANES:].astype(BF16)
        state = lax.dot_general(k, v, (((0,), (0,)), ((), ())), preferred_element_type=F32)
        state_ref[h * dim : (h + 1) * dim, :] = state[:dim]
        sent_ref[h * dim : (h + 1) * dim, :] = state[:dim].astype(BF16)


def query_kernel(heads, normed_ref, w_ref, q_ref, gate_ref):
    for h in range(heads):
        u = normed_ref[h]
        q = jnp.dot(u, w_ref[h, :, :LANES], preferred_element_type=F32)
        q_ref[h] = jnp.maximum(q, 0.0).astype(BF16)
        gate_ref[h] = jax.nn.sigmoid(jnp.dot(u, w_ref[h, :, 3 * LANES :], preferred_element_type=F32))


def finish_kernel(heads, dim, taken, place_ref, mixed_ref, q_ref, gate_ref, state_ref, *refs):
    got_refs, out_ref = refs[:-1], refs[-1]
    place = place_ref[0]
    for h in range(heads):
        rows = slice(h * dim, (h + 1) * dim)
        state = state_ref[rows, :]
        for i, got_ref in enumerate(got_refs):
            state = state + jnp.where(taken(place, i), got_ref[rows, :].astype(F32), 0.0)
        state = jnp.concatenate([state, jnp.zeros((LANES - dim, LANES), F32)], axis=0)
        new = finish(mixed_ref[h].astype(F32), gate_ref[h], attend(q_ref[h], state), dim)
        out_ref[:, h * dim : (h + 1) * dim] = new[:, :dim]


def exchange_rounds(state, sent, axis):
    size = lax.axis_size(axis)
    paired = size & (size - 1) == 0
    got = []
    total = state
    step = 1
    while step < size:
        if paired:
            partners = [(i, i ^ step) for i in range(size)]
        else:
            partners = [(i, i + step) for i in range(size - step)]
        got.append(lax.ppermute(sent, axis, partners))
        step *= 2
        if step < size:
            total = total + got[-1].astype(F32)
            sent = total.astype(BF16)

    def taken(place, turn):
        return (place >> turn) & 1 == 1 if paired else place >= 1 << turn

    return got, taken


def body(latents, spatial_weights, causal_weights):
    frames, rows, cols, width = latents.shape
    maps, all_heads, dim, _ = spatial_weights.shape
    n_row = lax.axis_size("row")
    if frames != 1 or n_row != 2 or dim > LANES:
        raise ValueError("unsupported shapes")
    heads = all_heads // n_row
    band = frames * rows * cols
    tokens = n_row * band
    row = jnp.reshape(lax.axis_index("row"), (1,)).astype(jnp.int32)
    place = jnp.reshape(lax.axis_index("frame"), (1,)).astype(jnp.int32)
    swap = [(i, n_row - 1 - i) for i in range(n_row)]

    own = latents.reshape(band, width)
    other = lax.ppermute(own, "row", swap)

    packed = jax.ShapeDtypeStruct((heads, LANES, maps * LANES), BF16)
    ws, wc = call(
        functools.partial(pack_kernel, heads), "pack", [packed, packed],
        [row, spatial_weights, causal_weights], [SMEM, VMEM, VMEM],
    )

    head_bf16 = jax.ShapeDtypeStruct((heads, tokens, LANES), BF16)
    head_f32 = jax.ShapeDtypeStruct((heads, tokens, LANES), F32)
    token_f32 = jax.ShapeDtypeStruct((tokens, LANES), F32)
    mixed, part = call(
        functools.partial(spatial_kernel, heads, dim, n_row), "spatial", [head_bf16, token_f32],
        [row, own, other, ws], [SMEM, VMEM, VMEM, VMEM],
        [pltpu.VMEM((heads, tokens, LANES), BF16), pltpu.VMEM((tokens, LANES), F32)],
        flops=2 * tokens * heads * LANES * LANES * 6,
    )
    part_other = lax.ppermute(part, "row", swap)

    normed, state, sent = call(
        functools.partial(state_kernel, heads, dim, width), "state",
        [head_bf16, jax.ShapeDtypeStruct((heads * dim, LANES), F32), jax.ShapeDtypeStruct((heads * dim, LANES), BF16)],
        [mixed, part, part_other, wc], [VMEM] * 4,
        flops=2 * tokens * heads * LANES * LANES * 3,
    )
    got, taken = exchange_rounds(state, sent, "frame")
    q, gate = call(
        functools.partial(query_kernel, heads), "query", [head_bf16, head_f32],
        [normed, wc], [VMEM, VMEM],
        flops=2 * tokens * heads * LANES * LANES * 2,
    )
    (out,) = call(
        functools.partial(finish_kernel, heads, dim, taken), "finish",
        [jax.ShapeDtypeStruct((tokens, heads * dim), BF16)],
        [place, mixed, q, gate, state, *got], [SMEM] + [VMEM] * (4 + len(got)),
        flops=2 * tokens * heads * LANES * LANES,
    )
    return out.reshape(frames, n_row * rows, cols, heads * dim)


def solution(mesh):
    in_specs = (P(("group", "frame"), "row", None, None), P(), P())
    out_specs = P(("group", "frame"), None, None, "row")
    return jax.shard_map(body, mesh=mesh, in_specs=in_specs, out_specs=out_specs, check_vma=False)
```

```python
import functools

import jax
import jax.numpy as jnp
from jax import lax
from jax.experimental import pallas as pl
from jax.experimental.pallas import tpu as pltpu
from jax.sharding import PartitionSpec as P

LANES = 128
SUBLANES = 8
F32 = jnp.float32
BF16 = jnp.bfloat16
VMEM = pl.BlockSpec(memory_space=pltpu.VMEM)
SMEM = pl.BlockSpec(memory_space=pltpu.SMEM)
HBM = pl.BlockSpec(memory_space=pltpu.HBM)


def call(kernel, name, outs, operands, in_specs, scratch=(), flops=0, limit=16 << 20, out_specs=None, aliases=None):
    n_bytes = sum(o.size * o.dtype.itemsize for o in operands)
    n_bytes += sum(o.size * o.dtype.itemsize for o in outs)
    return pl.pallas_call(
        kernel,
        name=name,
        out_shape=tuple(outs),
        in_specs=in_specs,
        out_specs=tuple(out_specs or [VMEM for _ in outs]),
        scratch_shapes=list(scratch),
        input_output_aliases=aliases or {},
        compiler_params=pltpu.CompilerParams(vmem_limit_bytes=limit),
        cost_estimate=pl.CostEstimate(flops=flops, bytes_accessed=n_bytes, transcendentals=0),
    )(*operands)


def fetch_maps(heads, row, w_hbm, w_ref, sems):
    first = row * heads
    copies = []
    for m in range(w_hbm.shape[0]):
        copies.append(pltpu.make_async_copy(w_hbm.at[m, pl.ds(first, heads)], w_ref.at[m], sems.at[m]))
        copies[-1].start()
    return copies


def pack_maps(heads, first, w_ref, out_ref, copies=()):
    dim = w_ref.shape[2]
    if dim < LANES:
        out_ref[:, dim:, :] = jnp.zeros((heads, LANES - dim, out_ref.shape[2]), BF16)
    for m in range(w_ref.shape[0]):
        if copies:
            copies[m].wait()
        for h in range(heads):
            block = w_ref[m, first + h]
            if dim < LANES:
                block = jnp.concatenate([block, jnp.zeros((dim, LANES - dim), BF16)], axis=1)
            out_ref[h, :dim, m * LANES : (m + 1) * LANES] = block


def split_heads(heads, dim, n_row, row, src_ref, u_ref, x_ref, at):
    band, width = src_ref.shape
    full = src_ref[...].astype(F32)
    inv = lax.rsqrt(jnp.sum(full * full, axis=-1, keepdims=True) / width + 1e-06)
    inv = jnp.broadcast_to(inv, (band, LANES))
    for r in range(n_row):

        @pl.when(row == r)
        def _():
            for h in range(heads):
                lo = (r * heads + h) * dim
                x = src_ref[:, lo : lo + dim]
                if dim < LANES:
                    x = jnp.concatenate([x, jnp.zeros((band, LANES - dim), BF16)], axis=1)
                x_ref[h, at, :] = x

    for h in range(heads):
        u_ref[h, at, :] = (x_ref[h, at, :].astype(F32) * inv).astype(BF16)


def lead_kernel(heads, dim, n_row, row_ref, own_hbm, w_hbm, u_ref, x_ref, maps_ref, own_ref, w_ref, sems):
    row = row_ref[0]
    mine = pltpu.make_async_copy(own_hbm, own_ref, sems.at[w_hbm.shape[0]])
    mine.start()
    copies = fetch_maps(heads, row, w_hbm, w_ref, sems)
    mine.wait()
    split_heads(heads, dim, n_row, row, own_ref, u_ref, x_ref, slice(None))
    pack_maps(heads, 0, w_ref, maps_ref, copies)


def pack_kernel(heads, row_ref, w_ref, maps_ref):
    pack_maps(heads, row_ref[0] * heads, w_ref, maps_ref)


def lane_blocks(sums, extra):
    blocks = sums.shape[0] // SUBLANES
    lane = lax.broadcasted_iota(jnp.int32, (SUBLANES, LANES), 1)
    tile = jnp.zeros((SUBLANES, LANES), F32)
    for b in range(blocks):
        here = lane == b
        if b < extra:
            here = jnp.logical_or(here, lane == blocks + b)
        tile = jnp.where(here, sums[b * SUBLANES : (b + 1) * SUBLANES, :], tile)
    return tile


def split_state(state):
    high = state.astype(BF16)
    low = (state - high.astype(F32)).astype(BF16)
    return jnp.concatenate([high, low], axis=0)


def attend(q, parts):
    return jnp.dot(jnp.concatenate([q, q], axis=1), parts, preferred_element_type=F32)


def finish(x, gate, attended, dim):
    inv_rms = lax.rsqrt(jnp.sum(attended * attended, axis=-1, keepdims=True) / dim + 1e-05)
    return (x + gate * attended * inv_rms).astype(BF16)


def outer_sum(k, v):
    return lax.dot_general(k, v, (((0,), (0,)), ((), ())), preferred_element_type=F32)


def spatial_kernel(
    heads, dim, n_row, row_ref, u_own_ref, x_own_ref, other_ref, w_ref,
    mixed_ref, part_ref, u_ref, x_ref, q_ref, k_ref, v_ref, gate_ref, parts_ref,
):
    band = other_ref.shape[0]
    split_heads(heads, dim, n_row, row_ref[0], other_ref, u_ref, x_ref, slice(None))
    for h in range(heads):
        u = jnp.concatenate([u_own_ref[h], u_ref[h]], axis=0)
        mapped = jnp.dot(u, w_ref[h], preferred_element_type=F32)
        q_ref[h] = jnp.maximum(mapped[:, :LANES], 0.0).astype(BF16)
        k_ref[h] = jnp.maximum(mapped[:, LANES : 2 * LANES], 0.0).astype(BF16)
        v_ref[h] = mapped[:, 2 * LANES : 3 * LANES].astype(BF16)
        gate_ref[h] = jax.nn.sigmoid(mapped[:, 3 * LANES :])
    for h in range(heads):
        parts_ref[h] = split_state(outer_sum(k_ref[h], v_ref[h]))
    part = jnp.zeros((2 * band, LANES), F32)
    for h in range(heads):
        x = jnp.concatenate([x_own_ref[h], x_ref[h]], axis=0).astype(F32)
        mixed = finish(x, gate_ref[h], attend(q_ref[h], parts_ref[h]), dim)
        mixed_ref[h] = mixed
        wide = mixed.astype(F32)
        part = part + wide * wide
    part_ref[...] = lane_blocks(jnp.sum(part, axis=-1, keepdims=True), band // SUBLANES)


def state_kernel(heads, dim, width, mixed_ref, part_ref, got_ref, w_ref, u_ref, parts_ref, sent_ref, k_ref, v_ref):
    blocks = mixed_ref.shape[1] // SUBLANES
    total = part_ref[...] + pltpu.roll(got_ref[...], LANES - blocks // 2, 1)
    tile = lax.rsqrt(total / width + 1e-06)
    inv = jnp.concatenate([jnp.broadcast_to(tile[:, b : b + 1], (SUBLANES, LANES)) for b in range(blocks)], axis=0)
    for h in range(heads):
        u = (mixed_ref[h].astype(F32) * inv).astype(BF16)
        u_ref[h] = u
        mapped = jnp.dot(u, w_ref[h, :, LANES : 3 * LANES], preferred_element_type=F32)
        k_ref[h] = jnp.maximum(mapped[:, :LANES], 0.0).astype(BF16)
        v_ref[h] = mapped[:, LANES:].astype(BF16)
    for h in range(heads):
        state = outer_sum(k_ref[h], v_ref[h])
        parts_ref[h] = split_state(state)
        store_packed(sent_ref, h, heads, dim, state[:dim].astype(BF16))


def packing(heads, dim):
    spare = LANES - dim
    if heads > 1 and spare and dim % spare == 0:
        for left in range(dim - 16, 0, -16):
            if (heads - 1) * (dim // left) >= dim // spare:
                return dim - left
    return dim


def packed_rows(heads, dim):
    return (heads - 1) * dim + packing(heads, dim)


def spare_blocks(heads, dim):
    kept = packing(heads, dim)
    left, spare = dim - kept, LANES - dim
    if not left:
        return []
    each = dim // left
    return [((c // each) * dim + (c % each) * left, c * spare) for c in range(dim // spare)]


def store_packed(ref, h, heads, dim, block):
    at = h * dim
    if h < heads - 1:
        ref[at : at + dim, :dim] = block[:, :dim]
        return
    kept = packing(heads, dim)
    ref[at : at + kept, :] = block[:kept]
    for row, lane in spare_blocks(heads, dim):
        ref[row : row + dim - kept, dim:] = block[kept:, lane : lane + LANES - dim]


def load_packed(ref, h, heads, dim, tail_ref):
    at = h * dim
    if h < heads - 1:
        block = ref[at : at + dim, :]
    else:
        kept = packing(heads, dim)
        tail_ref[:kept, :] = ref[at : at + kept, :]
        for row, lane in spare_blocks(heads, dim):
            tail_ref[kept:dim, lane : lane + LANES - dim] = ref[row : row + dim - kept, dim:]
        block = tail_ref[:dim, :]
    lane = lax.broadcasted_iota(jnp.int32, (dim, LANES), 1)
    block = jnp.where(lane < dim, block.astype(F32), 0.0)
    if dim < LANES:
        block = jnp.concatenate([block, jnp.zeros((LANES - dim, LANES), F32)], axis=0)
    return block


def write_out(heads, dim, n_row, row, mixed_ref, gate_ref, attended_ref, out_hbm, out_ref, sems):
    band = mixed_ref.shape[1] // n_row
    copies = []
    for b, place in enumerate((row, n_row - 1 - row)):
        at = slice(b * band, (b + 1) * band)
        for h in range(heads):
            new = finish(mixed_ref[h, at, :].astype(F32), gate_ref[h, at, :], attended_ref[h, at, :], dim)
            out_ref[at, h * dim : (h + 1) * dim] = new[:, :dim]
        to = pl.ds(pl.multiple_of(place * band, band), band)
        copies.append(pltpu.make_async_copy(out_ref.at[at], out_hbm.at[to], sems.at[b]))
        copies[-1].start()
    for copy in copies:
        copy.wait()


def query_kernel(heads, dim, n_row, taken, row_ref, place_ref, mixed_ref, u_ref, w_ref, parts_ref, *refs):
    got_refs, (q_ref, gate_ref, base_ref, out_hbm, out_ref, sum_ref, tail_ref, sems) = refs[:-8], refs[-8:]
    place = place_ref[0]
    if got_refs:
        earlier = jnp.zeros(sum_ref.shape, F32)
        for turn, got_ref in enumerate(got_refs):
            earlier = earlier + jnp.where(taken(place, turn), got_ref[...].astype(F32), 0.0)
        sum_ref[...] = earlier
    for h in range(heads):
        u = u_ref[h]
        q = jnp.maximum(jnp.dot(u, w_ref[h, :, :LANES], preferred_element_type=F32), 0.0).astype(BF16)
        q_ref[h] = q
        gate_ref[h] = jax.nn.sigmoid(jnp.dot(u, w_ref[h, :, 3 * LANES :], preferred_element_type=F32))
    for h in range(heads):
        base = attend(q_ref[h], parts_ref[h])
        if got_refs:
            base = base + attend(q_ref[h], split_state(load_packed(sum_ref, h, heads, dim, tail_ref)))
        base_ref[h] = base
    write_out(heads, dim, n_row, row_ref[0], mixed_ref, gate_ref, base_ref, out_hbm, out_ref, sems)


def finish_kernel(
    heads, dim, n_row, taken, turn, row_ref, place_ref, mixed_ref, q_ref, gate_ref, base_ref, got_ref, first_hbm,
    out_hbm, out_ref, state_ref, tail_ref, attended_ref, sems,
):
    @pl.when(taken(place_ref[0], turn))
    def _():
        for h in range(heads):
            state_ref[h] = load_packed(got_ref, h, heads, dim, tail_ref).astype(BF16)
        for h in range(heads):
            attended_ref[h] = base_ref[h] + jnp.dot(q_ref[h], state_ref[h], preferred_element_type=F32)
        write_out(heads, dim, n_row, row_ref[0], mixed_ref, gate_ref, attended_ref, out_hbm, out_ref, sems)


def exchange_rounds(sent, axis):
    size = lax.axis_size(axis)
    paired = size & (size - 1) == 0
    got = []
    total = sent.astype(F32)
    step = 1
    while step < size:
        if paired:
            partners = [(i, i ^ step) for i in range(size)]
        else:
            partners = [(i, i + step) for i in range(size - step)]
        got.append(lax.ppermute(sent, axis, partners))
        step *= 2
        if step < size:
            total = total + got[-1].astype(F32)
            sent = total.astype(BF16)

    def taken(place, turn):
        return (place >> turn) & 1 == 1 if paired else place >= 1 << turn

    return got, taken


def body(latents, spatial_weights, causal_weights):
    frames, rows, cols, width = latents.shape
    maps, all_heads, dim, _ = spatial_weights.shape
    n_row = lax.axis_size("row")
    if frames != 1 or n_row != 2 or dim > LANES or 3 * rows * cols > SUBLANES * LANES or lax.axis_size("frame") < 2:
        raise ValueError("unsupported shapes")
    heads = all_heads // n_row
    band = rows * cols
    tokens = n_row * band
    row = jnp.reshape(lax.axis_index("row"), (1,)).astype(jnp.int32)
    place = jnp.reshape(lax.axis_index("frame"), (1,)).astype(jnp.int32)
    swap = [(i, n_row - 1 - i) for i in range(n_row)]

    def shape(*dims, kind=BF16):
        return jax.ShapeDtypeStruct(dims, kind)

    packed_maps = shape(heads, LANES, maps * LANES)
    fetched = pltpu.VMEM((maps, heads, dim, dim), BF16)
    per_head = pltpu.VMEM((heads, tokens, LANES), BF16)
    band_head = pltpu.VMEM((heads, band, LANES), BF16)
    gates = pltpu.VMEM((heads, tokens, LANES), F32)

    own = latents.reshape(band, width)
    own_hbm = pltpu.with_memory_space_constraint(own, pltpu.HBM)
    spatial_weights = pltpu.with_memory_space_constraint(spatial_weights, pltpu.HBM)
    other = lax.ppermute(own, "row", swap)
    u_own, x_own, maps_s = call(
        functools.partial(lead_kernel, heads, dim, n_row), "lead",
        [shape(heads, band, LANES), shape(heads, band, LANES), packed_maps],
        [row, own_hbm, spatial_weights], [SMEM, HBM, HBM],
        [pltpu.VMEM((band, width), BF16), fetched, pltpu.SemaphoreType.DMA((maps + 1,))],
    )
    mixed, part = call(
        functools.partial(spatial_kernel, heads, dim, n_row), "spatial",
        [shape(heads, tokens, LANES), shape(SUBLANES, LANES, kind=F32)],
        [row, u_own, x_own, other, maps_s], [SMEM] + [VMEM] * 4,
        [band_head, band_head, per_head, per_head, per_head, gates, pltpu.VMEM((heads, 2 * LANES, LANES), BF16)],
        flops=2 * tokens * heads * LANES * LANES * 6,
    )
    causal_weights, part = lax.optimization_barrier((causal_weights, part))
    got_part = lax.ppermute(part, "row", swap)
    (maps_c,) = call(
        functools.partial(pack_kernel, heads), "pack", [packed_maps], [row, causal_weights], [SMEM, VMEM],
    )
    u, parts, sent = call(
        functools.partial(state_kernel, heads, dim, width), "state",
        [shape(heads, tokens, LANES), shape(heads, 2 * LANES, LANES), shape(packed_rows(heads, dim), LANES)],
        [mixed, part, got_part, maps_c], [VMEM] * 4, [per_head, per_head],
        flops=2 * tokens * heads * LANES * LANES * 3,
    )
    got, taken = exchange_rounds(sent, "frame")
    packed_sum = pltpu.VMEM((packed_rows(heads, dim), LANES), F32)
    whole = shape(tokens, heads * dim)
    writing = [pltpu.VMEM((tokens, heads * dim), BF16)]
    done = [pltpu.SemaphoreType.DMA((n_row,))]
    q, gate, base, out = call(
        functools.partial(query_kernel, heads, dim, n_row, taken), "query",
        [shape(heads, tokens, LANES), shape(heads, tokens, LANES, kind=F32), shape(heads, tokens, LANES, kind=F32), whole],
        [row, place, mixed, u, maps_c, parts, *got[:-1]], [SMEM] * 2 + [VMEM] * (3 + len(got)),
        writing + [packed_sum, pltpu.VMEM((LANES, LANES), F32)] + done,
        flops=2 * tokens * heads * LANES * LANES * 4, out_specs=[VMEM] * 3 + [HBM],
    )
    (out,) = call(
        functools.partial(finish_kernel, heads, dim, n_row, taken, len(got) - 1), "finish", [whole],
        [row, place, mixed, q, gate, base, got[-1], out], [SMEM] * 2 + [VMEM] * 5 + [HBM],
        writing + [pltpu.VMEM((heads, LANES, LANES), BF16), pltpu.VMEM((LANES, LANES), BF16), gates] + done,
        flops=2 * tokens * heads * LANES * LANES, out_specs=[HBM], aliases={7: 0},
    )
    return out.reshape(frames, n_row * rows, cols, heads * dim)


def solution(mesh):
    in_specs = (P(("group", "frame"), "row", None, None), P(), P())
    out_specs = P(("group", "frame"), None, None, "row")
    return jax.shard_map(body, mesh=mesh, in_specs=in_specs, out_specs=out_specs, check_vma=False)
```

```python
import functools

import jax
import jax.numpy as jnp
from jax import lax
from jax.experimental import pallas as pl
from jax.experimental.pallas import tpu as pltpu
from jax.sharding import PartitionSpec as P

LANES = 128
SUBLANES = 8
F32 = jnp.float32
BF16 = jnp.bfloat16
VMEM = pl.BlockSpec(memory_space=pltpu.VMEM)
SMEM = pl.BlockSpec(memory_space=pltpu.SMEM)
HBM = pl.BlockSpec(memory_space=pltpu.HBM)


def call(kernel, name, outs, operands, in_specs, scratch=(), flops=0, limit=16 << 20, out_specs=None, aliases=None):
    n_bytes = sum(o.size * o.dtype.itemsize for o in operands)
    n_bytes += sum(o.size * o.dtype.itemsize for o in outs)
    return pl.pallas_call(
        kernel,
        name=name,
        out_shape=tuple(outs),
        in_specs=in_specs,
        out_specs=tuple(out_specs or [VMEM for _ in outs]),
        scratch_shapes=list(scratch),
        input_output_aliases=aliases or {},
        compiler_params=pltpu.CompilerParams(vmem_limit_bytes=limit),
        cost_estimate=pl.CostEstimate(flops=flops, bytes_accessed=n_bytes, transcendentals=0),
    )(*operands)


def fetch_maps(heads, row, w_hbm, w_ref, sems):
    first = row * heads
    copies = []
    for m in range(w_hbm.shape[0]):
        copies.append(pltpu.make_async_copy(w_hbm.at[m, pl.ds(first, heads)], w_ref.at[m], sems.at[m]))
        copies[-1].start()
    return copies


def pack_maps(heads, first, w_ref, out_ref, copies=()):
    dim = w_ref.shape[2]
    if dim < LANES:
        out_ref[:, dim:, :] = jnp.zeros((heads, LANES - dim, out_ref.shape[2]), BF16)
    for m in range(w_ref.shape[0]):
        if copies:
            copies[m].wait()
        for h in range(heads):
            block = w_ref[m, first + h]
            if dim < LANES:
                block = jnp.concatenate([block, jnp.zeros((dim, LANES - dim), BF16)], axis=1)
            out_ref[h, :dim, m * LANES : (m + 1) * LANES] = block


def split_heads(heads, dim, n_row, row, src_ref, u_ref, x_ref, at):
    band, width = src_ref.shape
    full = src_ref[...].astype(F32)
    inv = lax.rsqrt(jnp.sum(full * full, axis=-1, keepdims=True) / width + 1e-06)
    inv = jnp.broadcast_to(inv, (band, LANES))
    for r in range(n_row):

        @pl.when(row == r)
        def _():
            for h in range(heads):
                lo = (r * heads + h) * dim
                x = src_ref[:, lo : lo + dim]
                if dim < LANES:
                    x = jnp.concatenate([x, jnp.zeros((band, LANES - dim), BF16)], axis=1)
                x_ref[h, at, :] = x

    for h in range(heads):
        u_ref[h, at, :] = (x_ref[h, at, :].astype(F32) * inv).astype(BF16)


def lead_kernel(heads, dim, n_row, row_ref, own_hbm, w_hbm, u_ref, x_ref, maps_ref, own_ref, w_ref, sems):
    row = row_ref[0]
    mine = pltpu.make_async_copy(own_hbm, own_ref, sems.at[w_hbm.shape[0]])
    mine.start()
    copies = fetch_maps(heads, row, w_hbm, w_ref, sems)
    mine.wait()
    split_heads(heads, dim, n_row, row, own_ref, u_ref, x_ref, slice(None))
    pack_maps(heads, 0, w_ref, maps_ref, copies)


def pack_kernel(heads, row_ref, w_ref, maps_ref):
    pack_maps(heads, row_ref[0] * heads, w_ref, maps_ref)


def lane_blocks(sums, extra):
    blocks = sums.shape[0] // SUBLANES
    lane = lax.broadcasted_iota(jnp.int32, (SUBLANES, LANES), 1)
    tile = jnp.zeros((SUBLANES, LANES), F32)
    for b in range(blocks):
        here = lane == b
        if b < extra:
            here = jnp.logical_or(here, lane == blocks + b)
        tile = jnp.where(here, sums[b * SUBLANES : (b + 1) * SUBLANES, :], tile)
    return tile


def split_state(state):
    high = state.astype(BF16)
    low = (state - high.astype(F32)).astype(BF16)
    return jnp.concatenate([high, low], axis=0)


def attend(q, parts):
    return jnp.dot(jnp.concatenate([q, q], axis=1), parts, preferred_element_type=F32)


def finish(x, gate, attended, dim):
    inv_rms = lax.rsqrt(jnp.sum(attended * attended, axis=-1, keepdims=True) / dim + 1e-05)
    return (x + gate * attended * inv_rms).astype(BF16)


def outer_sum(k, v):
    return lax.dot_general(k, v, (((0,), (0,)), ((), ())), preferred_element_type=F32)


def spatial_kernel(
    heads, dim, n_row, row_ref, u_own_ref, x_own_ref, other_ref, w_ref,
    mixed_ref, part_ref, u_ref, x_ref, q_ref, k_ref, v_ref, gate_ref, parts_ref,
):
    band = other_ref.shape[0]
    split_heads(heads, dim, n_row, row_ref[0], other_ref, u_ref, x_ref, slice(None))
    for h in range(heads):
        u = jnp.concatenate([u_own_ref[h], u_ref[h]], axis=0)
        mapped = jnp.dot(u, w_ref[h], preferred_element_type=F32)
        q_ref[h] = jnp.maximum(mapped[:, :LANES], 0.0).astype(BF16)
        k_ref[h] = jnp.maximum(mapped[:, LANES : 2 * LANES], 0.0).astype(BF16)
        v_ref[h] = mapped[:, 2 * LANES : 3 * LANES].astype(BF16)
        gate_ref[h] = jax.nn.sigmoid(mapped[:, 3 * LANES :])
    for h in range(heads):
        parts_ref[h] = split_state(outer_sum(k_ref[h], v_ref[h]))
    part = jnp.zeros((2 * band, LANES), F32)
    for h in range(heads):
        x = jnp.concatenate([x_own_ref[h], x_ref[h]], axis=0).astype(F32)
        mixed = finish(x, gate_ref[h], attend(q_ref[h], parts_ref[h]), dim)
        mixed_ref[h] = mixed
        wide = mixed.astype(F32)
        part = part + wide * wide
    part_ref[...] = lane_blocks(jnp.sum(part, axis=-1, keepdims=True), band // SUBLANES)


def state_kernel(heads, dim, width, mixed_ref, part_ref, got_ref, w_ref, u_ref, parts_ref, sent_ref, k_ref, v_ref):
    blocks = mixed_ref.shape[1] // SUBLANES
    total = part_ref[...] + pltpu.roll(got_ref[...], LANES - blocks // 2, 1)
    tile = lax.rsqrt(total / width + 1e-06)
    inv = jnp.concatenate([jnp.broadcast_to(tile[:, b : b + 1], (SUBLANES, LANES)) for b in range(blocks)], axis=0)
    for h in range(heads):
        u = (mixed_ref[h].astype(F32) * inv).astype(BF16)
        u_ref[h] = u
        mapped = jnp.dot(u, w_ref[h, :, LANES : 3 * LANES], preferred_element_type=F32)
        k_ref[h] = jnp.maximum(mapped[:, :LANES], 0.0).astype(BF16)
        v_ref[h] = mapped[:, LANES:].astype(BF16)
    for h in range(heads):
        state = outer_sum(k_ref[h], v_ref[h])
        parts_ref[h] = split_state(state)
        store_packed(sent_ref, h, heads, dim, state[:dim].astype(BF16))


def packing(heads, dim):
    spare = LANES - dim
    if heads > 1 and spare and dim % spare == 0:
        for left in range(dim - 16, 0, -16):
            if (heads - 1) * (dim // left) >= dim // spare:
                return dim - left
    return dim


def packed_rows(heads, dim):
    return (heads - 1) * dim + packing(heads, dim)


def spare_blocks(heads, dim):
    kept = packing(heads, dim)
    left, spare = dim - kept, LANES - dim
    if not left:
        return []
    each = dim // left
    return [((c // each) * dim + (c % each) * left, c * spare) for c in range(dim // spare)]


def store_packed(ref, h, heads, dim, block):
    at = h * dim
    if h < heads - 1:
        ref[at : at + dim, :dim] = block[:, :dim]
        return
    kept = packing(heads, dim)
    ref[at : at + kept, :] = block[:kept]
    for row, lane in spare_blocks(heads, dim):
        ref[row : row + dim - kept, dim:] = block[kept:, lane : lane + LANES - dim]


def load_packed(ref, h, heads, dim, tail_ref):
    at = h * dim
    if h < heads - 1:
        block = ref[at : at + dim, :]
    else:
        kept = packing(heads, dim)
        tail_ref[:kept, :] = ref[at : at + kept, :]
        for row, lane in spare_blocks(heads, dim):
            tail_ref[kept:dim, lane : lane + LANES - dim] = ref[row : row + dim - kept, dim:]
        block = tail_ref[:dim, :]
    lane = lax.broadcasted_iota(jnp.int32, (dim, LANES), 1)
    block = jnp.where(lane < dim, block.astype(F32), 0.0)
    if dim < LANES:
        block = jnp.concatenate([block, jnp.zeros((LANES - dim, LANES), F32)], axis=0)
    return block


def write_out(heads, dim, n_row, row, mixed_ref, gate_ref, attended_ref, out_hbm, out_ref, sems):
    band = mixed_ref.shape[1] // n_row
    for h in range(heads):
        new = finish(mixed_ref[h].astype(F32), gate_ref[h], attended_ref[h], dim)
        out_ref[:, h * dim : (h + 1) * dim] = new[:, :dim]
    copies = []
    for b, place in enumerate((row, n_row - 1 - row)):
        to = pl.ds(pl.multiple_of(place * band, band), band)
        copies.append(pltpu.make_async_copy(out_ref.at[b * band : (b + 1) * band], out_hbm.at[to], sems.at[b]))
        copies[-1].start()
    for copy in copies:
        copy.wait()


def query_kernel(heads, dim, n_row, taken, row_ref, place_ref, mixed_ref, u_ref, w_ref, parts_ref, *refs):
    got_refs, (q_ref, gate_ref, base_ref, out_hbm, out_ref, sum_ref, tail_ref, sems) = refs[:-8], refs[-8:]
    place = place_ref[0]
    if got_refs:
        earlier = jnp.zeros(sum_ref.shape, F32)
        for turn, got_ref in enumerate(got_refs):
            earlier = earlier + jnp.where(taken(place, turn), got_ref[...].astype(F32), 0.0)
        sum_ref[...] = earlier
    for h in range(heads):
        u = u_ref[h]
        q = jnp.maximum(jnp.dot(u, w_ref[h, :, :LANES], preferred_element_type=F32), 0.0).astype(BF16)
        q_ref[h] = q
        gate_ref[h] = jax.nn.sigmoid(jnp.dot(u, w_ref[h, :, 3 * LANES :], preferred_element_type=F32))
    for h in range(heads):
        base = attend(q_ref[h], parts_ref[h])
        if got_refs:
            base = base + attend(q_ref[h], split_state(load_packed(sum_ref, h, heads, dim, tail_ref)))
        base_ref[h] = base
    write_out(heads, dim, n_row, row_ref[0], mixed_ref, gate_ref, base_ref, out_hbm, out_ref, sems)


def finish_kernel(
    heads, dim, n_row, taken, turn, row_ref, place_ref, mixed_ref, q_ref, gate_ref, base_ref, got_ref, first_hbm,
    out_hbm, out_ref, state_ref, tail_ref, attended_ref, sems,
):
    @pl.when(taken(place_ref[0], turn))
    def _():
        for h in range(heads):
            state_ref[h] = load_packed(got_ref, h, heads, dim, tail_ref).astype(BF16)
        for h in range(heads):
            attended_ref[h] = base_ref[h] + jnp.dot(q_ref[h], state_ref[h], preferred_element_type=F32)
        write_out(heads, dim, n_row, row_ref[0], mixed_ref, gate_ref, attended_ref, out_hbm, out_ref, sems)


def exchange_rounds(sent, axis):
    size = lax.axis_size(axis)
    if size & (size - 1):
        raise ValueError("unsupported mesh")
    got, masks = [], []
    total = sent.astype(F32)
    block = 1
    while block < size:
        if 4 * block <= size:
            turn = [3 * block, 2 * block, block]
        else:
            turn = [block + block // 2]
        arrived = [lax.ppermute(sent, axis, [(i, i ^ mask) for i in range(size)]) for mask in turn]
        got += arrived
        masks += turn
        block *= len(turn) + 1
        if block < size:
            for one in arrived:
                total = total + one.astype(F32)
            sent = total.astype(BF16)

    def taken(place, turn):
        return (place >> (masks[turn].bit_length() - 1)) & 1 == 1

    return got, taken


def body(latents, spatial_weights, causal_weights):
    frames, rows, cols, width = latents.shape
    maps, all_heads, dim, _ = spatial_weights.shape
    n_row = lax.axis_size("row")
    if frames != 1 or n_row != 2 or dim > LANES or 3 * rows * cols > SUBLANES * LANES or lax.axis_size("frame") < 2:
        raise ValueError("unsupported shapes")
    heads = all_heads // n_row
    band = rows * cols
    tokens = n_row * band
    row = jnp.reshape(lax.axis_index("row"), (1,)).astype(jnp.int32)
    place = jnp.reshape(lax.axis_index("frame"), (1,)).astype(jnp.int32)
    swap = [(i, n_row - 1 - i) for i in range(n_row)]

    def shape(*dims, kind=BF16):
        return jax.ShapeDtypeStruct(dims, kind)

    packed_maps = shape(heads, LANES, maps * LANES)
    fetched = pltpu.VMEM((maps, heads, dim, dim), BF16)
    per_head = pltpu.VMEM((heads, tokens, LANES), BF16)
    band_head = pltpu.VMEM((heads, band, LANES), BF16)
    gates = pltpu.VMEM((heads, tokens, LANES), F32)

    own = latents.reshape(band, width)
    own_hbm = pltpu.with_memory_space_constraint(own, pltpu.HBM)
    spatial_weights = pltpu.with_memory_space_constraint(spatial_weights, pltpu.HBM)
    other = lax.ppermute(own, "row", swap)
    u_own, x_own, maps_s = call(
        functools.partial(lead_kernel, heads, dim, n_row), "lead",
        [shape(heads, band, LANES), shape(heads, band, LANES), packed_maps],
        [row, own_hbm, spatial_weights], [SMEM, HBM, HBM],
        [pltpu.VMEM((band, width), BF16), fetched, pltpu.SemaphoreType.DMA((maps + 1,))],
    )
    mixed, part = call(
        functools.partial(spatial_kernel, heads, dim, n_row), "spatial",
        [shape(heads, tokens, LANES), shape(SUBLANES, LANES, kind=F32)],
        [row, u_own, x_own, other, maps_s], [SMEM] + [VMEM] * 4,
        [band_head, band_head, per_head, per_head, per_head, gates, pltpu.VMEM((heads, 2 * LANES, LANES), BF16)],
        flops=2 * tokens * heads * LANES * LANES * 6,
    )
    causal_weights, part = lax.optimization_barrier((causal_weights, part))
    got_part = lax.ppermute(part, "row", swap)
    (maps_c,) = call(
        functools.partial(pack_kernel, heads), "pack", [packed_maps], [row, causal_weights], [SMEM, VMEM],
    )
    u, parts, sent = call(
        functools.partial(state_kernel, heads, dim, width), "state",
        [shape(heads, tokens, LANES), shape(heads, 2 * LANES, LANES), shape(packed_rows(heads, dim), LANES)],
        [mixed, part, got_part, maps_c], [VMEM] * 4, [per_head, per_head],
        flops=2 * tokens * heads * LANES * LANES * 3,
    )
    got, taken = exchange_rounds(sent, "frame")
    packed_sum = pltpu.VMEM((packed_rows(heads, dim), LANES), F32)
    whole = shape(tokens, heads * dim)
    writing = [pltpu.VMEM((tokens, heads * dim), BF16)]
    done = [pltpu.SemaphoreType.DMA((n_row,))]
    q, gate, base, out = call(
        functools.partial(query_kernel, heads, dim, n_row, taken), "query",
        [shape(heads, tokens, LANES), shape(heads, tokens, LANES, kind=F32), shape(heads, tokens, LANES, kind=F32), whole],
        [row, place, mixed, u, maps_c, parts, *got[:-1]], [SMEM] * 2 + [VMEM] * (3 + len(got)),
        writing + [packed_sum, pltpu.VMEM((LANES, LANES), F32)] + done,
        flops=2 * tokens * heads * LANES * LANES * 4, out_specs=[VMEM] * 3 + [HBM],
    )
    (out,) = call(
        functools.partial(finish_kernel, heads, dim, n_row, taken, len(got) - 1), "finish", [whole],
        [row, place, mixed, q, gate, base, got[-1], out], [SMEM] * 2 + [VMEM] * 5 + [HBM],
        writing + [pltpu.VMEM((heads, LANES, LANES), BF16), pltpu.VMEM((LANES, LANES), BF16), gates] + done,
        flops=2 * tokens * heads * LANES * LANES, out_specs=[HBM], aliases={7: 0},
    )
    return out.reshape(frames, n_row * rows, cols, heads * dim)


def solution(mesh):
    in_specs = (P(("group", "frame"), "row", None, None), P(), P())
    out_specs = P(("group", "frame"), None, None, "row")
    return jax.shard_map(body, mesh=mesh, in_specs=in_specs, out_specs=out_specs, check_vma=False)
```

```python
import functools

import jax
import jax.numpy as jnp
from jax import lax
from jax.experimental import pallas as pl
from jax.experimental.pallas import tpu as pltpu
from jax.sharding import PartitionSpec as P

LANES = 128
SUBLANES = 8
F32 = jnp.float32
BF16 = jnp.bfloat16
VMEM = pl.BlockSpec(memory_space=pltpu.VMEM)
SMEM = pl.BlockSpec(memory_space=pltpu.SMEM)
HBM = pl.BlockSpec(memory_space=pltpu.HBM)


def call(kernel, name, outs, operands, in_specs, scratch=(), flops=0, limit=16 << 20, out_specs=None, aliases=None):
    n_bytes = sum(o.size * o.dtype.itemsize for o in operands)
    n_bytes += sum(o.size * o.dtype.itemsize for o in outs)
    return pl.pallas_call(
        kernel,
        name=name,
        out_shape=tuple(outs),
        in_specs=in_specs,
        out_specs=tuple(out_specs or [VMEM for _ in outs]),
        scratch_shapes=list(scratch),
        input_output_aliases=aliases or {},
        compiler_params=pltpu.CompilerParams(vmem_limit_bytes=limit),
        cost_estimate=pl.CostEstimate(flops=flops, bytes_accessed=n_bytes, transcendentals=0),
    )(*operands)


def fetch_maps(heads, row, w_hbm, w_ref, sems):
    first = row * heads
    copies = []
    for m in range(w_hbm.shape[0]):
        copies.append(pltpu.make_async_copy(w_hbm.at[m, pl.ds(first, heads)], w_ref.at[m], sems.at[m]))
        copies[-1].start()
    return copies


def pack_maps(heads, first, w_ref, out_ref, copies=()):
    dim = w_ref.shape[2]
    if dim < LANES:
        out_ref[:, dim:, :] = jnp.zeros((heads, LANES - dim, out_ref.shape[2]), BF16)
    for m in range(w_ref.shape[0]):
        if copies:
            copies[m].wait()
        for h in range(heads):
            block = w_ref[m, first + h]
            if dim < LANES:
                block = jnp.concatenate([block, jnp.zeros((dim, LANES - dim), BF16)], axis=1)
            out_ref[h, :dim, m * LANES : (m + 1) * LANES] = block


def split_heads(heads, dim, n_row, row, src_ref, u_ref, x_ref):
    band, width = src_ref.shape
    full = src_ref[...].astype(F32)
    inv = lax.rsqrt(jnp.sum(full * full, axis=-1, keepdims=True) / width + 1e-06)
    inv = jnp.broadcast_to(inv, (band, LANES))
    for r in range(n_row):

        @pl.when(row == r)
        def _():
            for h in range(heads):
                lo = (r * heads + h) * dim
                x = src_ref[:, lo : lo + dim]
                if dim < LANES:
                    x = jnp.concatenate([x, jnp.zeros((band, LANES - dim), BF16)], axis=1)
                x_ref[h] = x

    for h in range(heads):
        u_ref[h] = (x_ref[h].astype(F32) * inv).astype(BF16)


def project(heads, u_ref, maps_ref, q_ref, k_ref, v_ref, gate_ref):
    for h in range(heads):
        mapped = jnp.dot(u_ref[h], maps_ref[h], preferred_element_type=F32)
        q_ref[h] = jnp.maximum(mapped[:, :LANES], 0.0).astype(BF16)
        k_ref[h] = jnp.maximum(mapped[:, LANES : 2 * LANES], 0.0).astype(BF16)
        v_ref[h] = mapped[:, 2 * LANES : 3 * LANES].astype(BF16)
        gate_ref[h] = jax.nn.sigmoid(mapped[:, 3 * LANES :])


def lead_kernel(
    heads, dim, n_row, row_ref, own_hbm, w_hbm,
    x_ref, q_ref, k_ref, v_ref, gate_ref, maps_ref, u_ref, own_ref, w_ref, sems,
):
    row = row_ref[0]
    mine = pltpu.make_async_copy(own_hbm, own_ref, sems.at[w_hbm.shape[0]])
    mine.start()
    copies = fetch_maps(heads, row, w_hbm, w_ref, sems)
    mine.wait()
    split_heads(heads, dim, n_row, row, own_ref, u_ref, x_ref)
    pack_maps(heads, 0, w_ref, maps_ref, copies)
    project(heads, u_ref, maps_ref, q_ref, k_ref, v_ref, gate_ref)


def lane_blocks(sums, extra):
    blocks = sums.shape[0] // SUBLANES
    lane = lax.broadcasted_iota(jnp.int32, (SUBLANES, LANES), 1)
    tile = jnp.zeros((SUBLANES, LANES), F32)
    for b in range(blocks):
        here = lane == b
        if b < extra:
            here = jnp.logical_or(here, lane == blocks + b)
        tile = jnp.where(here, sums[b * SUBLANES : (b + 1) * SUBLANES, :], tile)
    return tile


def split_state(state):
    high = state.astype(BF16)
    low = (state - high.astype(F32)).astype(BF16)
    return jnp.concatenate([high, low], axis=0)


def attend(q, parts):
    return jnp.dot(jnp.concatenate([q, q], axis=1), parts, preferred_element_type=F32)


def finish(x, gate, attended, dim):
    inv_rms = lax.rsqrt(jnp.sum(attended * attended, axis=-1, keepdims=True) / dim + 1e-05)
    return (x + gate * attended * inv_rms).astype(BF16)


def outer_sum(k, v):
    return lax.dot_general(k, v, (((0,), (0,)), ((), ())), preferred_element_type=F32)


def stacked(first_ref, then_ref, h):
    return jnp.concatenate([first_ref[h], then_ref[h]], axis=0)


def spatial_kernel(
    heads, dim, n_row, row_ref, x_own_ref, q_own_ref, k_own_ref, v_own_ref, gate_own_ref, other_ref, maps_ref,
    mixed_ref, part_ref, u_ref, x_ref, q_ref, k_ref, v_ref, gate_ref, parts_ref,
):
    band = other_ref.shape[0]
    split_heads(heads, dim, n_row, row_ref[0], other_ref, u_ref, x_ref)
    project(heads, u_ref, maps_ref, q_ref, k_ref, v_ref, gate_ref)
    for h in range(heads):
        parts_ref[h] = split_state(outer_sum(stacked(k_own_ref, k_ref, h), stacked(v_own_ref, v_ref, h)))
    part = jnp.zeros((2 * band, LANES), F32)
    for h in range(heads):
        attended = attend(stacked(q_own_ref, q_ref, h), parts_ref[h])
        mixed = finish(stacked(x_own_ref, x_ref, h).astype(F32), stacked(gate_own_ref, gate_ref, h), attended, dim)
        mixed_ref[h] = mixed
        wide = mixed.astype(F32)
        part = part + wide * wide
    part_ref[...] = lane_blocks(jnp.sum(part, axis=-1, keepdims=True), band // SUBLANES)


def token_scale(width, blocks, part_ref, got_ref):
    total = part_ref[...] + pltpu.roll(got_ref[...], LANES - blocks // 2, 1)
    tile = lax.rsqrt(total / width + 1e-06)
    return jnp.concatenate([jnp.broadcast_to(tile[:, b : b + 1], (SUBLANES, LANES)) for b in range(blocks)], axis=0)


def early_kernel(heads, row_ref, mixed_ref, w_ref, maps_ref, k_ref, v_ref):
    pack_maps(heads, row_ref[0] * heads, w_ref, maps_ref)
    for h in range(heads):
        mapped = jnp.dot(mixed_ref[h], maps_ref[h, :, LANES : 3 * LANES], preferred_element_type=F32)
        k_ref[h] = jnp.maximum(mapped[:, :LANES], 0.0)
        v_ref[h] = mapped[:, LANES:]


def state_kernel(heads, dim, width, k_ref, v_ref, part_ref, got_ref, state_ref, sent_ref):
    inv = token_scale(width, k_ref.shape[1] // SUBLANES, part_ref, got_ref)
    for h in range(heads):
        state = outer_sum((k_ref[h] * inv).astype(BF16), (v_ref[h] * inv).astype(BF16))
        state_ref[h] = state
        store_packed(sent_ref, h, heads, dim, state[:dim].astype(BF16))


def packing(heads, dim):
    spare = LANES - dim
    if heads > 1 and spare and dim % spare == 0:
        for left in range(dim - 16, 0, -16):
            if (heads - 1) * (dim // left) >= dim // spare:
                return dim - left
    return dim


def packed_rows(heads, dim):
    return (heads - 1) * dim + packing(heads, dim)


def spare_blocks(heads, dim):
    kept = packing(heads, dim)
    left, spare = dim - kept, LANES - dim
    if not left:
        return []
    each = dim // left
    return [((c // each) * dim + (c % each) * left, c * spare) for c in range(dim // spare)]


def store_packed(ref, h, heads, dim, block):
    at = h * dim
    if h < heads - 1:
        ref[at : at + dim, :dim] = block[:, :dim]
        return
    kept = packing(heads, dim)
    ref[at : at + kept, :] = block[:kept]
    for row, lane in spare_blocks(heads, dim):
        ref[row : row + dim - kept, dim:] = block[kept:, lane : lane + LANES - dim]


def load_packed(ref, h, heads, dim, tail_ref):
    at = h * dim
    if h < heads - 1:
        block = ref[at : at + dim, :]
    else:
        kept = packing(heads, dim)
        tail_ref[:kept, :] = ref[at : at + kept, :]
        for row, lane in spare_blocks(heads, dim):
            tail_ref[kept:dim, lane : lane + LANES - dim] = ref[row : row + dim - kept, dim:]
        block = tail_ref[:dim, :]
    lane = lax.broadcasted_iota(jnp.int32, (dim, LANES), 1)
    block = jnp.where(lane < dim, block.astype(F32), 0.0)
    if dim < LANES:
        block = jnp.concatenate([block, jnp.zeros((LANES - dim, LANES), F32)], axis=0)
    return block


def write_out(heads, dim, n_row, row, mixed_ref, gate_ref, attended_ref, out_hbm, out_ref, sems):
    band = mixed_ref.shape[1] // n_row
    for h in range(heads):
        new = finish(mixed_ref[h].astype(F32), gate_ref[h], attended_ref[h], dim)
        out_ref[:, h * dim : (h + 1) * dim] = new[:, :dim]
    copies = []
    for b, place in enumerate((row, n_row - 1 - row)):
        to = pl.ds(pl.multiple_of(place * band, band), band)
        copies.append(pltpu.make_async_copy(out_ref.at[b * band : (b + 1) * band], out_hbm.at[to], sems.at[b]))
        copies[-1].start()
    for copy in copies:
        copy.wait()


def query_kernel(
    heads, dim, width, n_row, taken, row_ref, place_ref, mixed_ref, part_ref, got_part_ref, maps_ref, state_ref, *refs
):
    got_refs, (q_ref, gate_ref, base_ref, out_hbm, out_ref, sum_ref, tail_ref, sems) = refs[:-8], refs[-8:]
    place = place_ref[0]
    earlier = jnp.zeros(sum_ref.shape, F32)
    for turn, got_ref in enumerate(got_refs):
        earlier = earlier + jnp.where(taken(place, turn), got_ref[...].astype(F32), 0.0)
    sum_ref[...] = earlier
    inv = token_scale(width, mixed_ref.shape[1] // SUBLANES, part_ref, got_part_ref)
    for h in range(heads):
        u = (mixed_ref[h].astype(F32) * inv).astype(BF16)
        q = jnp.maximum(jnp.dot(u, maps_ref[h, :, :LANES], preferred_element_type=F32), 0.0).astype(BF16)
        q_ref[h] = q
        gate_ref[h] = jax.nn.sigmoid(jnp.dot(u, maps_ref[h, :, 3 * LANES :], preferred_element_type=F32))
    for h in range(heads):
        state = state_ref[h]
        if got_refs:
            state = state + load_packed(sum_ref, h, heads, dim, tail_ref)
        base_ref[h] = attend(q_ref[h], split_state(state))
    write_out(heads, dim, n_row, row_ref[0], mixed_ref, gate_ref, base_ref, out_hbm, out_ref, sems)


def finish_kernel(
    heads, dim, n_row, taken, turn, row_ref, place_ref, mixed_ref, q_ref, gate_ref, base_ref, got_ref, first_hbm,
    out_hbm, out_ref, state_ref, tail_ref, attended_ref, sems,
):
    @pl.when(taken(place_ref[0], turn))
    def _():
        for h in range(heads):
            state_ref[h] = load_packed(got_ref, h, heads, dim, tail_ref).astype(BF16)
        for h in range(heads):
            attended_ref[h] = base_ref[h] + jnp.dot(q_ref[h], state_ref[h], preferred_element_type=F32)
        write_out(heads, dim, n_row, row_ref[0], mixed_ref, gate_ref, attended_ref, out_hbm, out_ref, sems)


def exchange_rounds(sent, axis):
    size = lax.axis_size(axis)
    if size & (size - 1):
        raise ValueError("unsupported mesh")
    got, masks = [], []
    total = sent.astype(F32)
    block = 1
    while block < size:
        if 4 * block <= size:
            turn = [3 * block, 2 * block, block]
        else:
            turn = [block + block // 2]
        arrived = [lax.ppermute(sent, axis, [(i, i ^ mask) for i in range(size)]) for mask in turn]
        got += arrived
        masks += turn
        block *= len(turn) + 1
        if block < size:
            for one in arrived:
                total = total + one.astype(F32)
            sent = total.astype(BF16)

    def taken(place, turn):
        return (place >> (masks[turn].bit_length() - 1)) & 1 == 1

    return got, taken


def body(latents, spatial_weights, causal_weights):
    frames, rows, cols, width = latents.shape
    maps, all_heads, dim, _ = spatial_weights.shape
    n_row = lax.axis_size("row")
    if frames != 1 or n_row != 2 or dim > LANES or 3 * rows * cols > SUBLANES * LANES or lax.axis_size("frame") < 2:
        raise ValueError("unsupported shapes")
    heads = all_heads // n_row
    band = rows * cols
    tokens = n_row * band
    row = jnp.reshape(lax.axis_index("row"), (1,)).astype(jnp.int32)
    place = jnp.reshape(lax.axis_index("frame"), (1,)).astype(jnp.int32)
    swap = [(i, n_row - 1 - i) for i in range(n_row)]

    def shape(*dims, kind=BF16):
        return jax.ShapeDtypeStruct(dims, kind)

    packed_maps = shape(heads, LANES, maps * LANES)
    fetched = pltpu.VMEM((maps, heads, dim, dim), BF16)
    band_head = pltpu.VMEM((heads, band, LANES), BF16)
    band_gates = pltpu.VMEM((heads, band, LANES), F32)
    gates = pltpu.VMEM((heads, tokens, LANES), F32)
    own_outs = [shape(heads, band, LANES)] * 4 + [shape(heads, band, LANES, kind=F32)]
    head_flops = 2 * tokens * heads * LANES * LANES

    own = latents.reshape(band, width)
    own_hbm = pltpu.with_memory_space_constraint(own, pltpu.HBM)
    spatial_weights = pltpu.with_memory_space_constraint(spatial_weights, pltpu.HBM)
    other = lax.ppermute(own, "row", swap)
    *of_own, maps_s = call(
        functools.partial(lead_kernel, heads, dim, n_row), "lead", own_outs + [packed_maps],
        [row, own_hbm, spatial_weights], [SMEM, HBM, HBM],
        [band_head, pltpu.VMEM((band, width), BF16), fetched, pltpu.SemaphoreType.DMA((maps + 1,))],
        flops=head_flops * 2,
    )
    mixed, part = call(
        functools.partial(spatial_kernel, heads, dim, n_row), "spatial",
        [shape(heads, tokens, LANES), shape(SUBLANES, LANES, kind=F32)],
        [row, *of_own, other, maps_s], [SMEM] + [VMEM] * 7,
        [band_head] * 5 + [band_gates, pltpu.VMEM((heads, 2 * LANES, LANES), BF16)],
        flops=head_flops * 4,
    )
    got_part = lax.ppermute(part, "row", swap)
    maps_c, k, v = call(
        functools.partial(early_kernel, heads), "early",
        [packed_maps] + [shape(heads, tokens, LANES, kind=F32)] * 2,
        [row, mixed, causal_weights], [SMEM, VMEM, VMEM], flops=head_flops * 2,
    )
    state, sent = call(
        functools.partial(state_kernel, heads, dim, width), "state",
        [shape(heads, LANES, LANES, kind=F32), shape(packed_rows(heads, dim), LANES)],
        [k, v, part, got_part], [VMEM] * 4, flops=head_flops,
    )
    got, taken = exchange_rounds(sent, "frame")
    packed_sum = pltpu.VMEM((packed_rows(heads, dim), LANES), F32)
    whole = shape(tokens, heads * dim)
    writing = [pltpu.VMEM((tokens, heads * dim), BF16)]
    done = [pltpu.SemaphoreType.DMA((n_row,))]
    q, gate, base, out = call(
        functools.partial(query_kernel, heads, dim, width, n_row, taken), "query",
        [shape(heads, tokens, LANES), shape(heads, tokens, LANES, kind=F32), shape(heads, tokens, LANES, kind=F32), whole],
        [row, place, mixed, part, got_part, maps_c, state, *got[:-1]], [SMEM] * 2 + [VMEM] * (4 + len(got)),
        writing + [packed_sum, pltpu.VMEM((LANES, LANES), F32)] + done,
        flops=head_flops * 4, out_specs=[VMEM] * 3 + [HBM],
    )
    (out,) = call(
        functools.partial(finish_kernel, heads, dim, n_row, taken, len(got) - 1), "finish", [whole],
        [row, place, mixed, q, gate, base, got[-1], out], [SMEM] * 2 + [VMEM] * 5 + [HBM],
        writing + [pltpu.VMEM((heads, LANES, LANES), BF16), pltpu.VMEM((LANES, LANES), BF16), gates] + done,
        flops=head_flops, out_specs=[HBM], aliases={7: 0},
    )
    return out.reshape(frames, n_row * rows, cols, heads * dim)


def solution(mesh):
    in_specs = (P(("group", "frame"), "row", None, None), P(), P())
    out_specs = P(("group", "frame"), None, None, "row")
    return jax.shard_map(body, mesh=mesh, in_specs=in_specs, out_specs=out_specs, check_vma=False)
```

```python
import functools

import jax
import jax.numpy as jnp
from jax import lax
from jax.experimental import pallas as pl
from jax.experimental.pallas import tpu as pltpu
from jax.sharding import PartitionSpec as P

LANES = 128
SUBLANES = 8
F32 = jnp.float32
BF16 = jnp.bfloat16
VMEM = pl.BlockSpec(memory_space=pltpu.VMEM)
SMEM = pl.BlockSpec(memory_space=pltpu.SMEM)
HBM = pl.BlockSpec(memory_space=pltpu.HBM)


def call(kernel, name, outs, operands, in_specs, scratch=(), flops=0, limit=16 << 20, out_specs=None, aliases=None):
    n_bytes = sum(o.size * o.dtype.itemsize for o in operands)
    n_bytes += sum(o.size * o.dtype.itemsize for o in outs)
    return pl.pallas_call(
        kernel,
        name=name,
        out_shape=tuple(outs),
        in_specs=in_specs,
        out_specs=tuple(out_specs or [VMEM for _ in outs]),
        scratch_shapes=list(scratch),
        input_output_aliases=aliases or {},
        compiler_params=pltpu.CompilerParams(vmem_limit_bytes=limit),
        cost_estimate=pl.CostEstimate(flops=flops, bytes_accessed=n_bytes, transcendentals=0),
    )(*operands)


def split_heads(heads, dim, n_row, row, src_ref, u_ref, x_ref):
    band, width = src_ref.shape
    full = src_ref[...].astype(F32)
    inv = lax.rsqrt(jnp.sum(full * full, axis=-1, keepdims=True) / width + 1e-06)
    inv = jnp.broadcast_to(inv, (band, LANES))
    for r in range(n_row):

        @pl.when(row == r)
        def _():
            for h in range(heads):
                lo = (r * heads + h) * dim
                x_ref[h] = lanes_of(src_ref[:, lo : lo + dim])

    for h in range(heads):
        u_ref[h] = (x_ref[h].astype(F32) * inv).astype(BF16)


def project(heads, u_ref, maps_ref, q_ref, k_ref, v_ref, gate_ref):
    for h in range(heads):
        mapped = jnp.dot(u_ref[h], maps_ref[h], preferred_element_type=F32)
        q_ref[h] = jnp.maximum(mapped[:, :LANES], 0.0).astype(BF16)
        k_ref[h] = jnp.maximum(mapped[:, LANES : 2 * LANES], 0.0).astype(BF16)
        v_ref[h] = mapped[:, 2 * LANES : 3 * LANES].astype(BF16)
        gate_ref[h] = jax.nn.sigmoid(mapped[:, 3 * LANES :])


def lead_kernel(
    heads, dim, n_row, row_ref, own_hbm, w_hbm,
    x_ref, q_ref, k_ref, v_ref, gate_ref, maps_ref, u_ref, own_ref, w_ref, sems,
):
    row = row_ref[0]
    mine = pltpu.make_async_copy(own_hbm, own_ref, sems.at[0])
    mine.start()
    fetch = pltpu.make_async_copy(w_hbm.at[:, pl.ds(row * heads, heads)], w_ref, sems.at[1])
    fetch.start()
    clear_maps(heads, dim, maps_ref)
    mine.wait()
    split_heads(heads, dim, n_row, row, own_ref, u_ref, x_ref)
    fetch.wait()
    for m in range(w_ref.shape[0]):
        pack_map(heads, 0, m, w_ref, maps_ref)
    project(heads, u_ref, maps_ref, q_ref, k_ref, v_ref, gate_ref)


def lanes_of(block):
    rows, dim = block.shape
    return jnp.concatenate([block, jnp.zeros((rows, LANES - dim), block.dtype)], axis=1) if dim < LANES else block


def clear_maps(heads, dim, maps_ref):
    if dim < LANES:
        maps_ref[:, dim:, :] = jnp.zeros((heads, LANES - dim, maps_ref.shape[2]), BF16)


def pack_map(heads, first, m, w_ref, maps_ref):
    dim = w_ref.shape[2]
    for h in range(heads):
        maps_ref[h, :dim, m * LANES : (m + 1) * LANES] = lanes_of(w_ref[m, first + h])


def lane_blocks(sums, extra):
    blocks = sums.shape[0] // SUBLANES
    lane = lax.broadcasted_iota(jnp.int32, (SUBLANES, LANES), 1)
    tile = jnp.zeros((SUBLANES, LANES), F32)
    for b in range(blocks):
        here = lane == b
        if b < extra:
            here = jnp.logical_or(here, lane == blocks + b)
        tile = jnp.where(here, sums[b * SUBLANES : (b + 1) * SUBLANES, :], tile)
    return tile


def split_state(state):
    high = state.astype(BF16)
    low = (state - high.astype(F32)).astype(BF16)
    return jnp.concatenate([high, low], axis=0)


def attend(q, parts):
    return jnp.dot(jnp.concatenate([q, q], axis=1), parts, preferred_element_type=F32)


def finish(x, gate, attended, dim):
    inv_rms = lax.rsqrt(jnp.sum(attended * attended, axis=-1, keepdims=True) / dim + 1e-05)
    return (x + gate * attended * inv_rms).astype(BF16)


def outer_sum(k, v):
    return lax.dot_general(k, v, (((0,), (0,)), ((), ())), preferred_element_type=F32)


def stacked(first_ref, then_ref, h):
    return jnp.concatenate([first_ref[h], then_ref[h]], axis=0)


def spatial_kernel(
    heads, dim, n_row, row_ref, x_own_ref, q_own_ref, k_own_ref, v_own_ref, gate_own_ref, other_ref, maps_ref,
    mixed_ref, part_ref, u_ref, x_ref, q_ref, k_ref, v_ref, gate_ref, parts_ref,
):
    band = other_ref.shape[0]
    split_heads(heads, dim, n_row, row_ref[0], other_ref, u_ref, x_ref)
    project(heads, u_ref, maps_ref, q_ref, k_ref, v_ref, gate_ref)
    for h in range(heads):
        parts_ref[h] = split_state(outer_sum(stacked(k_own_ref, k_ref, h), stacked(v_own_ref, v_ref, h)))
    part = jnp.zeros((2 * band, LANES), F32)
    for h in range(heads):
        attended = attend(stacked(q_own_ref, q_ref, h), parts_ref[h])
        mixed = finish(stacked(x_own_ref, x_ref, h).astype(F32), stacked(gate_own_ref, gate_ref, h), attended, dim)
        mixed_ref[h] = mixed
        wide = mixed.astype(F32)
        part = part + wide * wide
    part_ref[...] = lane_blocks(jnp.sum(part, axis=-1, keepdims=True), band // SUBLANES)


def token_scale(width, blocks, part_ref, got_ref):
    total = part_ref[...] + pltpu.roll(got_ref[...], LANES - blocks // 2, 1)
    tile = lax.rsqrt(total / width + 1e-06)
    return jnp.concatenate([jnp.broadcast_to(tile[:, b : b + 1], (SUBLANES, LANES)) for b in range(blocks)], axis=0)


def early_kernel(heads, row_ref, mixed_ref, w_ref, maps_ref, k_ref, v_ref):
    clear_maps(heads, w_ref.shape[2], maps_ref)
    for m in range(w_ref.shape[0]):
        pack_map(heads, row_ref[0] * heads, m, w_ref, maps_ref)
    for h in range(heads):
        mapped = jnp.dot(mixed_ref[h], maps_ref[h, :, LANES : 3 * LANES], preferred_element_type=F32)
        k_ref[h] = jnp.maximum(mapped[:, :LANES], 0.0)
        v_ref[h] = mapped[:, LANES:]


def state_kernel(heads, dim, width, k_ref, v_ref, part_ref, got_ref, state_ref, sent_ref):
    inv = token_scale(width, k_ref.shape[1] // SUBLANES, part_ref, got_ref)
    for h in range(heads):
        state = outer_sum((k_ref[h] * inv).astype(BF16), (v_ref[h] * inv).astype(BF16))
        state_ref[h] = state
        store_packed(sent_ref, h, heads, dim, state[:dim].astype(BF16))


def packing(heads, dim):
    spare = LANES - dim
    if heads > 1 and spare and dim % spare == 0:
        for left in range((dim - 1) // 16 * 16, 0, -16):
            if dim // spare * left <= (heads - 1) * dim:
                return dim - left
    return dim


def packed_rows(heads, dim):
    return (heads - 1) * dim + packing(heads, dim)


def spare_blocks(heads, dim):
    left, spare = dim - packing(heads, dim), LANES - dim
    return [(c * left, c * spare) for c in range(dim // spare)] if left else []


def store_packed(ref, h, heads, dim, block):
    at = h * dim
    if h < heads - 1:
        ref[at : at + dim, :dim] = block[:, :dim]
        return
    kept = packing(heads, dim)
    ref[at : at + kept, :] = block[:kept]
    for row, lane in spare_blocks(heads, dim):
        ref[row : row + dim - kept, dim:] = block[kept:, lane : lane + LANES - dim]


def load_packed(ref, h, heads, dim, tail_ref):
    at = h * dim
    if h < heads - 1:
        block = ref[at : at + dim, :]
    else:
        kept = packing(heads, dim)
        tail_ref[:kept, :] = ref[at : at + kept, :]
        for row, lane in spare_blocks(heads, dim):
            tail_ref[kept:dim, lane : lane + LANES - dim] = ref[row : row + dim - kept, dim:]
        block = tail_ref[:dim, :]
    lane = lax.broadcasted_iota(jnp.int32, (dim, LANES), 1)
    block = jnp.where(lane < dim, block.astype(F32), 0.0)
    if dim < LANES:
        block = jnp.concatenate([block, jnp.zeros((LANES - dim, LANES), F32)], axis=0)
    return block


def write_out(heads, dim, n_row, row, mixed_ref, gate_ref, attended_ref, out_hbm, out_ref, sems):
    band = mixed_ref.shape[1] // n_row
    for h in range(heads):
        new = finish(mixed_ref[h].astype(F32), gate_ref[h], attended_ref[h], dim)
        out_ref[:, h * dim : (h + 1) * dim] = new[:, :dim]
    copies = []
    for b, place in enumerate((row, n_row - 1 - row)):
        to = pl.ds(pl.multiple_of(place * band, band), band)
        copies.append(pltpu.make_async_copy(out_ref.at[b * band : (b + 1) * band], out_hbm.at[to], sems.at[b]))
        copies[-1].start()
    for copy in copies:
        copy.wait()


def query_kernel(
    heads, dim, width, n_row, taken, row_ref, place_ref, mixed_ref, part_ref, got_part_ref, maps_ref, state_ref, *refs
):
    got_refs, (q_ref, gate_ref, base_ref, out_hbm, out_ref, sum_ref, tail_ref, sems) = refs[:-8], refs[-8:]
    place = place_ref[0]
    earlier = jnp.zeros(sum_ref.shape, F32)
    for turn, got_ref in enumerate(got_refs):
        earlier = earlier + jnp.where(taken(place, turn), got_ref[...].astype(F32), 0.0)
    sum_ref[...] = earlier
    inv = token_scale(width, mixed_ref.shape[1] // SUBLANES, part_ref, got_part_ref)
    for h in range(heads):
        u = (mixed_ref[h].astype(F32) * inv).astype(BF16)
        q = jnp.maximum(jnp.dot(u, maps_ref[h, :, :LANES], preferred_element_type=F32), 0.0).astype(BF16)
        q_ref[h] = q
        gate_ref[h] = jax.nn.sigmoid(jnp.dot(u, maps_ref[h, :, 3 * LANES :], preferred_element_type=F32))
    for h in range(heads):
        state = state_ref[h]
        if got_refs:
            state = state + load_packed(sum_ref, h, heads, dim, tail_ref)
        base_ref[h] = attend(q_ref[h], split_state(state))
    write_out(heads, dim, n_row, row_ref[0], mixed_ref, gate_ref, base_ref, out_hbm, out_ref, sems)


def finish_kernel(
    heads, dim, n_row, taken, turn, row_ref, place_ref, mixed_ref, q_ref, gate_ref, base_ref, got_ref, first_hbm,
    out_hbm, out_ref, state_ref, tail_ref, attended_ref, sems,
):
    @pl.when(taken(place_ref[0], turn))
    def _():
        for h in range(heads):
            state_ref[h] = load_packed(got_ref, h, heads, dim, tail_ref).astype(BF16)
        for h in range(heads):
            attended_ref[h] = base_ref[h] + jnp.dot(q_ref[h], state_ref[h], preferred_element_type=F32)
        write_out(heads, dim, n_row, row_ref[0], mixed_ref, gate_ref, attended_ref, out_hbm, out_ref, sems)


def exchange_rounds(sent, axis):
    size = lax.axis_size(axis)
    if size & (size - 1):
        raise ValueError("unsupported mesh")
    got, masks = [], []
    total = sent.astype(F32)
    block = 1
    while block < size:
        if 4 * block <= size:
            turn = [3 * block, 2 * block, block]
        else:
            turn = [block + block // 2]
        arrived = [lax.ppermute(sent, axis, [(i, i ^ mask) for i in range(size)]) for mask in turn]
        got += arrived
        masks += turn
        block *= len(turn) + 1
        if block < size:
            for one in arrived:
                total = total + one.astype(F32)
            sent = total.astype(BF16)

    def taken(place, turn):
        return (place >> (masks[turn].bit_length() - 1)) & 1 == 1

    return got, taken


def body(latents, spatial_weights, causal_weights):
    frames, rows, cols, width = latents.shape
    maps, all_heads, dim, _ = spatial_weights.shape
    n_row = lax.axis_size("row")
    if frames != 1 or n_row != 2 or dim > LANES or 3 * rows * cols > SUBLANES * LANES or lax.axis_size("frame") < 2:
        raise ValueError("unsupported shapes")
    heads = all_heads // n_row
    band = rows * cols
    tokens = n_row * band
    row = jnp.reshape(lax.axis_index("row"), (1,)).astype(jnp.int32)
    place = jnp.reshape(lax.axis_index("frame"), (1,)).astype(jnp.int32)
    swap = [(i, n_row - 1 - i) for i in range(n_row)]

    def shape(*dims, kind=BF16):
        return jax.ShapeDtypeStruct(dims, kind)

    packed_maps = shape(heads, LANES, maps * LANES)
    fetched = pltpu.VMEM((maps, heads, dim, dim), BF16)
    band_head = pltpu.VMEM((heads, band, LANES), BF16)
    band_gates = pltpu.VMEM((heads, band, LANES), F32)
    gates = pltpu.VMEM((heads, tokens, LANES), F32)
    own_outs = [shape(heads, band, LANES)] * 4 + [shape(heads, band, LANES, kind=F32)]
    head_flops = 2 * tokens * heads * LANES * LANES

    own = latents.reshape(band, width)
    own_hbm = pltpu.with_memory_space_constraint(own, pltpu.HBM)
    spatial_weights = pltpu.with_memory_space_constraint(spatial_weights, pltpu.HBM)
    other = lax.ppermute(own, "row", swap)
    *of_own, maps_s = call(
        functools.partial(lead_kernel, heads, dim, n_row), "lead", own_outs + [packed_maps],
        [row, own_hbm, spatial_weights], [SMEM, HBM, HBM],
        [band_head, pltpu.VMEM((band, width), BF16), fetched, pltpu.SemaphoreType.DMA((2,))],
        flops=head_flops * 2,
    )
    mixed, part = call(
        functools.partial(spatial_kernel, heads, dim, n_row), "spatial",
        [shape(heads, tokens, LANES), shape(SUBLANES, LANES, kind=F32)],
        [row, *of_own, other, maps_s], [SMEM] + [VMEM] * 7,
        [band_head] * 5 + [band_gates, pltpu.VMEM((heads, 2 * LANES, LANES), BF16)],
        flops=head_flops * 4,
    )
    got_part = lax.ppermute(part, "row", swap)
    maps_c, k, v = call(
        functools.partial(early_kernel, heads), "early",
        [packed_maps] + [shape(heads, tokens, LANES, kind=F32)] * 2,
        [row, mixed, causal_weights], [SMEM, VMEM, VMEM], flops=head_flops * 2,
    )
    state, sent = call(
        functools.partial(state_kernel, heads, dim, width), "state",
        [shape(heads, LANES, LANES, kind=F32), shape(packed_rows(heads, dim), LANES)],
        [k, v, part, got_part], [VMEM] * 4, flops=head_flops,
    )
    got, taken = exchange_rounds(sent, "frame")
    packed_sum = pltpu.VMEM((packed_rows(heads, dim), LANES), F32)
    whole = shape(tokens, heads * dim)
    writing = [pltpu.VMEM((tokens, heads * dim), BF16)]
    done = [pltpu.SemaphoreType.DMA((n_row,))]
    q, gate, base, out = call(
        functools.partial(query_kernel, heads, dim, width, n_row, taken), "query",
        [shape(heads, tokens, LANES), shape(heads, tokens, LANES, kind=F32), shape(heads, tokens, LANES, kind=F32), whole],
        [row, place, mixed, part, got_part, maps_c, state, *got[:-1]], [SMEM] * 2 + [VMEM] * (4 + len(got)),
        writing + [packed_sum, pltpu.VMEM((LANES, LANES), F32)] + done,
        flops=head_flops * 4, out_specs=[VMEM] * 3 + [HBM],
    )
    (out,) = call(
        functools.partial(finish_kernel, heads, dim, n_row, taken, len(got) - 1), "finish", [whole],
        [row, place, mixed, q, gate, base, got[-1], out], [SMEM] * 2 + [VMEM] * 5 + [HBM],
        writing + [pltpu.VMEM((heads, LANES, LANES), BF16), pltpu.VMEM((LANES, LANES), BF16), gates] + done,
        flops=head_flops, out_specs=[HBM], aliases={7: 0},
    )
    return out.reshape(frames, n_row * rows, cols, heads * dim)


def solution(mesh):
    in_specs = (P(("group", "frame"), "row", None, None), P(), P())
    out_specs = P(("group", "frame"), None, None, "row")
    return jax.shard_map(body, mesh=mesh, in_specs=in_specs, out_specs=out_specs, check_vma=False)
```

```python
import functools

import jax
import jax.numpy as jnp
from jax import lax
from jax.experimental import pallas as pl
from jax.experimental.pallas import tpu as pltpu
from jax.sharding import PartitionSpec as P

LANES = 128
SUBLANES = 8
F32 = jnp.float32
BF16 = jnp.bfloat16
VMEM = pl.BlockSpec(memory_space=pltpu.VMEM)
SMEM = pl.BlockSpec(memory_space=pltpu.SMEM)
HBM = pl.BlockSpec(memory_space=pltpu.HBM)


def call(kernel, name, outs, operands, in_specs, scratch=(), flops=0, limit=16 << 20, out_specs=None, aliases=None):
    n_bytes = sum(o.size * o.dtype.itemsize for o in operands)
    n_bytes += sum(o.size * o.dtype.itemsize for o in outs)
    return pl.pallas_call(
        kernel,
        name=name,
        out_shape=tuple(outs),
        in_specs=in_specs,
        out_specs=tuple(out_specs or [VMEM for _ in outs]),
        scratch_shapes=list(scratch),
        input_output_aliases=aliases or {},
        compiler_params=pltpu.CompilerParams(vmem_limit_bytes=limit),
        cost_estimate=pl.CostEstimate(flops=flops, bytes_accessed=n_bytes, transcendentals=0),
    )(*operands)


def split_heads(heads, dim, n_row, row, src_ref, u_ref, x_ref):
    band, width = src_ref.shape
    full = src_ref[...].astype(F32)
    inv = lax.rsqrt(jnp.sum(full * full, axis=-1, keepdims=True) / width + 1e-06)
    inv = jnp.broadcast_to(inv, (band, LANES))
    for r in range(n_row):

        @pl.when(row == r)
        def _():
            for h in range(heads):
                lo = (r * heads + h) * dim
                x_ref[h] = lanes_of(src_ref[:, lo : lo + dim])

    for h in range(heads):
        u_ref[h] = (x_ref[h].astype(F32) * inv).astype(BF16)


def project(heads, u_ref, maps_ref, q_ref, k_ref, v_ref, gate_ref):
    for h in range(heads):
        mapped = jnp.dot(u_ref[h], maps_ref[h, :, LANES : 3 * LANES], preferred_element_type=F32)
        k_ref[h] = jnp.maximum(mapped[:, :LANES], 0.0).astype(BF16)
        v_ref[h] = mapped[:, LANES:].astype(BF16)
    for h in range(heads):
        u = u_ref[h]
        q_ref[h] = jnp.maximum(jnp.dot(u, maps_ref[h, :, :LANES], preferred_element_type=F32), 0.0).astype(BF16)
        gate_ref[h] = jax.nn.sigmoid(jnp.dot(u, maps_ref[h, :, 3 * LANES :], preferred_element_type=F32))


def lead_kernel(
    heads, dim, n_row, row_ref, own_hbm, w_hbm,
    x_ref, q_ref, k_ref, v_ref, gate_ref, maps_ref, u_ref, own_ref, w_ref, sems,
):
    row = row_ref[0]
    mine = pltpu.make_async_copy(own_hbm, own_ref, sems.at[0])
    mine.start()
    fetch = pltpu.make_async_copy(w_hbm.at[:, pl.ds(row * heads, heads)], w_ref, sems.at[1])
    fetch.start()
    clear_maps(heads, dim, maps_ref)
    mine.wait()
    split_heads(heads, dim, n_row, row, own_ref, u_ref, x_ref)
    fetch.wait()
    for m in range(w_ref.shape[0]):
        pack_map(heads, 0, m, w_ref, maps_ref)
    project(heads, u_ref, maps_ref, q_ref, k_ref, v_ref, gate_ref)


def lanes_of(block):
    rows, dim = block.shape
    return jnp.concatenate([block, jnp.zeros((rows, LANES - dim), block.dtype)], axis=1) if dim < LANES else block


def clear_maps(heads, dim, maps_ref):
    if dim < LANES:
        maps_ref[:, dim:, :] = jnp.zeros((heads, LANES - dim, maps_ref.shape[2]), BF16)


def pack_map(heads, first, m, w_ref, maps_ref):
    dim = w_ref.shape[2]
    for h in range(heads):
        maps_ref[h, :dim, m * LANES : (m + 1) * LANES] = lanes_of(w_ref[m, first + h])


def lane_blocks(sums, extra):
    blocks = sums.shape[0] // SUBLANES
    lane = lax.broadcasted_iota(jnp.int32, (SUBLANES, LANES), 1)
    tile = jnp.zeros((SUBLANES, LANES), F32)
    for b in range(blocks):
        here = lane == b
        if b < extra:
            here = jnp.logical_or(here, lane == blocks + b)
        tile = jnp.where(here, sums[b * SUBLANES : (b + 1) * SUBLANES, :], tile)
    return tile


def split_state(state):
    high = state.astype(BF16)
    low = (state - high.astype(F32)).astype(BF16)
    return jnp.concatenate([high, low], axis=0)


def attend(q, parts):
    return jnp.dot(jnp.concatenate([q, q], axis=1), parts, preferred_element_type=F32)


def finish(x, gate, attended, dim):
    inv_rms = lax.rsqrt(jnp.sum(attended * attended, axis=-1, keepdims=True) / dim + 1e-05)
    return (x + gate * attended * inv_rms).astype(BF16)


def outer_sum(k, v):
    return lax.dot_general(k, v, (((0,), (0,)), ((), ())), preferred_element_type=F32)


def stacked(first_ref, then_ref, h):
    return jnp.concatenate([first_ref[h], then_ref[h]], axis=0)


def spatial_kernel(
    heads, dim, n_row, row_ref, x_own_ref, q_own_ref, k_own_ref, v_own_ref, gate_own_ref, other_ref, maps_ref,
    mixed_ref, part_ref, u_ref, x_ref, q_ref, k_ref, v_ref, gate_ref, parts_ref,
):
    band = other_ref.shape[0]
    split_heads(heads, dim, n_row, row_ref[0], other_ref, u_ref, x_ref)
    project(heads, u_ref, maps_ref, q_ref, k_ref, v_ref, gate_ref)
    for h in range(heads):
        parts_ref[h] = split_state(outer_sum(stacked(k_own_ref, k_ref, h), stacked(v_own_ref, v_ref, h)))
    part = jnp.zeros((2 * band, LANES), F32)
    for h in range(heads):
        attended = attend(stacked(q_own_ref, q_ref, h), parts_ref[h])
        mixed = finish(stacked(x_own_ref, x_ref, h).astype(F32), stacked(gate_own_ref, gate_ref, h), attended, dim)
        mixed_ref[h] = mixed
        wide = mixed.astype(F32)
        part = part + wide * wide
    part_ref[...] = lane_blocks(jnp.sum(part, axis=-1, keepdims=True), band // SUBLANES)


def token_scale(width, blocks, part_ref, got_ref):
    total = part_ref[...] + pltpu.roll(got_ref[...], LANES - blocks // 2, 1)
    tile = lax.rsqrt(total / width + 1e-06)
    return jnp.concatenate([jnp.broadcast_to(tile[:, b : b + 1], (SUBLANES, LANES)) for b in range(blocks)], axis=0)


def early_kernel(heads, row_ref, mixed_ref, w_ref, maps_ref, k_ref, v_ref):
    clear_maps(heads, w_ref.shape[2], maps_ref)
    for m in range(w_ref.shape[0]):
        pack_map(heads, row_ref[0] * heads, m, w_ref, maps_ref)
    for h in range(heads):
        mapped = jnp.dot(mixed_ref[h], maps_ref[h, :, LANES : 3 * LANES], preferred_element_type=F32)
        k_ref[h] = jnp.maximum(mapped[:, :LANES], 0.0)
        v_ref[h] = mapped[:, LANES:]


def state_kernel(heads, dim, width, k_ref, v_ref, part_ref, got_ref, state_ref, sent_ref):
    inv = token_scale(width, k_ref.shape[1] // SUBLANES, part_ref, got_ref)
    for h in range(heads):
        state = outer_sum((k_ref[h] * inv).astype(BF16), (v_ref[h] * inv).astype(BF16))
        state_ref[h] = state
        store_packed(sent_ref, h, heads, dim, state[:dim].astype(BF16))


def packing(heads, dim):
    spare = LANES - dim
    if heads > 1 and spare and dim % spare == 0:
        for left in range((dim - 1) // 16 * 16, 0, -16):
            if dim // spare * left <= (heads - 1) * dim:
                return dim - left
    return dim


def packed_rows(heads, dim):
    return (heads - 1) * dim + packing(heads, dim)


def spare_blocks(heads, dim):
    left, spare = dim - packing(heads, dim), LANES - dim
    return [(c * left, c * spare) for c in range(dim // spare)] if left else []


def store_packed(ref, h, heads, dim, block):
    at = h * dim
    if h < heads - 1:
        ref[at : at + dim, :dim] = block[:, :dim]
        return
    kept = packing(heads, dim)
    ref[at : at + kept, :] = block[:kept]
    for row, lane in spare_blocks(heads, dim):
        ref[row : row + dim - kept, dim:] = block[kept:, lane : lane + LANES - dim]


def load_packed(ref, h, heads, dim, tail_ref):
    at = h * dim
    if h < heads - 1:
        block = ref[at : at + dim, :]
    else:
        kept = packing(heads, dim)
        tail_ref[:kept, :] = ref[at : at + kept, :]
        for row, lane in spare_blocks(heads, dim):
            tail_ref[kept:dim, lane : lane + LANES - dim] = ref[row : row + dim - kept, dim:]
        block = tail_ref[:dim, :]
    lane = lax.broadcasted_iota(jnp.int32, (dim, LANES), 1)
    block = jnp.where(lane < dim, block.astype(F32), 0.0)
    if dim < LANES:
        block = jnp.concatenate([block, jnp.zeros((LANES - dim, LANES), F32)], axis=0)
    return block


def write_out(heads, dim, n_row, row, mixed_ref, gate_ref, attended_ref, scaled_ref, out_hbm, out_ref, sems):
    band = mixed_ref.shape[1] // n_row
    for h in range(heads):
        attended = attended_ref[h]
        scaled_ref[h] = attended * lax.rsqrt(jnp.sum(attended * attended, axis=-1, keepdims=True) / dim + 1e-05)
    copies = []
    for b, place in enumerate((row, n_row - 1 - row)):
        at = slice(b * band, (b + 1) * band)
        for h in range(heads):
            new = (mixed_ref[h, at, :].astype(F32) + gate_ref[h, at, :] * scaled_ref[h, at, :]).astype(BF16)
            out_ref[at, h * dim : (h + 1) * dim] = new[:, :dim]
        to = pl.ds(pl.multiple_of(place * band, band), band)
        copies.append(pltpu.make_async_copy(out_ref.at[at], out_hbm.at[to], sems.at[b]))
        copies[-1].start()
    for copy in copies:
        copy.wait()


def query_kernel(
    heads, dim, width, n_row, taken, row_ref, place_ref, mixed_ref, part_ref, got_part_ref, maps_ref, state_ref, *refs
):
    got_refs, (q_ref, gate_ref, base_ref, out_hbm, out_ref, scaled_ref, sum_ref, tail_ref, sems) = refs[:-9], refs[-9:]
    place = place_ref[0]
    earlier = jnp.zeros(sum_ref.shape, F32)
    for turn, got_ref in enumerate(got_refs):
        earlier = earlier + jnp.where(taken(place, turn), got_ref[...].astype(F32), 0.0)
    sum_ref[...] = earlier
    inv = token_scale(width, mixed_ref.shape[1] // SUBLANES, part_ref, got_part_ref)
    for h in range(heads):
        u = (mixed_ref[h].astype(F32) * inv).astype(BF16)
        q = jnp.maximum(jnp.dot(u, maps_ref[h, :, :LANES], preferred_element_type=F32), 0.0).astype(BF16)
        q_ref[h] = q
        gate_ref[h] = jax.nn.sigmoid(jnp.dot(u, maps_ref[h, :, 3 * LANES :], preferred_element_type=F32))
    for h in range(heads):
        state = state_ref[h]
        if got_refs:
            state = state + load_packed(sum_ref, h, heads, dim, tail_ref)
        base_ref[h] = attend(q_ref[h], split_state(state))
    write_out(heads, dim, n_row, row_ref[0], mixed_ref, gate_ref, base_ref, scaled_ref, out_hbm, out_ref, sems)


def finish_kernel(
    heads, dim, n_row, taken, turn, row_ref, place_ref, mixed_ref, q_ref, gate_ref, base_ref, got_ref, first_hbm,
    out_hbm, out_ref, state_ref, tail_ref, attended_ref, sems,
):
    @pl.when(taken(place_ref[0], turn))
    def _():
        for h in range(heads):
            state_ref[h] = load_packed(got_ref, h, heads, dim, tail_ref).astype(BF16)
        for h in range(heads):
            attended_ref[h] = base_ref[h] + jnp.dot(q_ref[h], state_ref[h], preferred_element_type=F32)
        write_out(
            heads, dim, n_row, row_ref[0], mixed_ref, gate_ref, attended_ref, attended_ref, out_hbm, out_ref, sems
        )


def exchange_rounds(sent, axis):
    size = lax.axis_size(axis)
    if size & (size - 1):
        raise ValueError("unsupported mesh")
    got, masks = [], []
    total = sent.astype(F32)
    block = 1
    while block < size:
        if 4 * block <= size:
            turn = [3 * block, 2 * block, block]
        else:
            turn = [block + block // 2]
        arrived = [lax.ppermute(sent, axis, [(i, i ^ mask) for i in range(size)]) for mask in turn]
        got += arrived
        masks += turn
        block *= len(turn) + 1
        if block < size:
            for one in arrived:
                total = total + one.astype(F32)
            sent = total.astype(BF16)

    def taken(place, turn):
        return (place >> (masks[turn].bit_length() - 1)) & 1 == 1

    return got, taken


def body(latents, spatial_weights, causal_weights):
    frames, rows, cols, width = latents.shape
    maps, all_heads, dim, _ = spatial_weights.shape
    n_row = lax.axis_size("row")
    if frames != 1 or n_row != 2 or dim > LANES or 3 * rows * cols > SUBLANES * LANES or lax.axis_size("frame") < 2:
        raise ValueError("unsupported shapes")
    heads = all_heads // n_row
    band = rows * cols
    tokens = n_row * band
    row = jnp.reshape(lax.axis_index("row"), (1,)).astype(jnp.int32)
    place = jnp.reshape(lax.axis_index("frame"), (1,)).astype(jnp.int32)
    swap = [(i, n_row - 1 - i) for i in range(n_row)]

    def shape(*dims, kind=BF16):
        return jax.ShapeDtypeStruct(dims, kind)

    packed_maps = shape(heads, LANES, maps * LANES)
    fetched = pltpu.VMEM((maps, heads, dim, dim), BF16)
    band_head = pltpu.VMEM((heads, band, LANES), BF16)
    band_gates = pltpu.VMEM((heads, band, LANES), F32)
    gates = pltpu.VMEM((heads, tokens, LANES), F32)
    own_outs = [shape(heads, band, LANES)] * 4 + [shape(heads, band, LANES, kind=F32)]
    head_flops = 2 * tokens * heads * LANES * LANES

    own = latents.reshape(band, width)
    own_hbm = pltpu.with_memory_space_constraint(own, pltpu.HBM)
    spatial_weights = pltpu.with_memory_space_constraint(spatial_weights, pltpu.HBM)
    other = lax.ppermute(own, "row", swap)
    *of_own, maps_s = call(
        functools.partial(lead_kernel, heads, dim, n_row), "lead", own_outs + [packed_maps],
        [row, own_hbm, spatial_weights], [SMEM, HBM, HBM],
        [band_head, pltpu.VMEM((band, width), BF16), fetched, pltpu.SemaphoreType.DMA((2,))],
        flops=head_flops * 2,
    )
    mixed, part = call(
        functools.partial(spatial_kernel, heads, dim, n_row), "spatial",
        [shape(heads, tokens, LANES), shape(SUBLANES, LANES, kind=F32)],
        [row, *of_own, other, maps_s], [SMEM] + [VMEM] * 7,
        [band_head] * 5 + [band_gates, pltpu.VMEM((heads, 2 * LANES, LANES), BF16)],
        flops=head_flops * 4,
    )
    got_part = lax.ppermute(part, "row", swap)
    maps_c, k, v = call(
        functools.partial(early_kernel, heads), "early",
        [packed_maps] + [shape(heads, tokens, LANES, kind=F32)] * 2,
        [row, mixed, causal_weights], [SMEM, VMEM, VMEM], flops=head_flops * 2,
    )
    state, sent = call(
        functools.partial(state_kernel, heads, dim, width), "state",
        [shape(heads, LANES, LANES, kind=F32), shape(packed_rows(heads, dim), LANES)],
        [k, v, part, got_part], [VMEM] * 4, flops=head_flops,
    )
    got, taken = exchange_rounds(sent, "frame")
    packed_sum = pltpu.VMEM((packed_rows(heads, dim), LANES), F32)
    whole = shape(tokens, heads * dim)
    writing = [pltpu.VMEM((tokens, heads * dim), BF16)]
    done = [pltpu.SemaphoreType.DMA((n_row,))]
    q, gate, base, out = call(
        functools.partial(query_kernel, heads, dim, width, n_row, taken), "query",
        [shape(heads, tokens, LANES), shape(heads, tokens, LANES, kind=F32), shape(heads, tokens, LANES, kind=F32), whole],
        [row, place, mixed, part, got_part, maps_c, state, *got[:-1]], [SMEM] * 2 + [VMEM] * (4 + len(got)),
        writing + [gates, packed_sum, pltpu.VMEM((LANES, LANES), F32)] + done,
        flops=head_flops * 4, out_specs=[VMEM] * 3 + [HBM],
    )
    (out,) = call(
        functools.partial(finish_kernel, heads, dim, n_row, taken, len(got) - 1), "finish", [whole],
        [row, place, mixed, q, gate, base, got[-1], out], [SMEM] * 2 + [VMEM] * 5 + [HBM],
        writing + [pltpu.VMEM((heads, LANES, LANES), BF16), pltpu.VMEM((LANES, LANES), BF16), gates] + done,
        flops=head_flops, out_specs=[HBM], aliases={7: 0},
    )
    return out.reshape(frames, n_row * rows, cols, heads * dim)


def solution(mesh):
    in_specs = (P(("group", "frame"), "row", None, None), P(), P())
    out_specs = P(("group", "frame"), None, None, "row")
    return jax.shard_map(body, mesh=mesh, in_specs=in_specs, out_specs=out_specs, check_vma=False)
```

```python
import functools

import jax
import jax.numpy as jnp
from jax import lax
from jax.experimental import pallas as pl
from jax.experimental.pallas import tpu as pltpu
from jax.sharding import PartitionSpec as P

LANES = 128
SUBLANES = 8
F32 = jnp.float32
BF16 = jnp.bfloat16
VMEM = pl.BlockSpec(memory_space=pltpu.VMEM)
SMEM = pl.BlockSpec(memory_space=pltpu.SMEM)
HBM = pl.BlockSpec(memory_space=pltpu.HBM)


def call(kernel, name, outs, operands, in_specs, scratch=(), flops=0, limit=16 << 20, out_specs=None, aliases=None):
    n_bytes = sum(o.size * o.dtype.itemsize for o in operands)
    n_bytes += sum(o.size * o.dtype.itemsize for o in outs)
    return pl.pallas_call(
        kernel,
        name=name,
        out_shape=tuple(outs),
        in_specs=in_specs,
        out_specs=tuple(out_specs or [VMEM for _ in outs]),
        scratch_shapes=list(scratch),
        input_output_aliases=aliases or {},
        compiler_params=pltpu.CompilerParams(vmem_limit_bytes=limit),
        cost_estimate=pl.CostEstimate(flops=flops, bytes_accessed=n_bytes, transcendentals=0),
    )(*operands)


def split_heads(heads, dim, n_row, row, src_ref, u_ref, x_ref):
    band, width = src_ref.shape
    full = src_ref[...].astype(F32)
    inv = lax.rsqrt(jnp.sum(full * full, axis=-1, keepdims=True) / width + 1e-06)
    inv = jnp.broadcast_to(inv, (band, LANES))
    for r in range(n_row):

        @pl.when(row == r)
        def _():
            for h in range(heads):
                lo = (r * heads + h) * dim
                x_ref[h] = lanes_of(src_ref[:, lo : lo + dim])

    for h in range(heads):
        u_ref[h] = (x_ref[h].astype(F32) * inv).astype(BF16)


def project(heads, u_ref, maps_ref, q_ref, k_ref, v_ref, gate_ref):
    for h in range(heads):
        mapped = jnp.dot(u_ref[h], maps_ref[h, :, LANES : 3 * LANES], preferred_element_type=F32)
        k_ref[h] = jnp.maximum(mapped[:, :LANES], 0.0).astype(BF16)
        v_ref[h] = mapped[:, LANES:].astype(BF16)
    for h in range(heads):
        u = u_ref[h]
        q_ref[h] = jnp.maximum(jnp.dot(u, maps_ref[h, :, :LANES], preferred_element_type=F32), 0.0).astype(BF16)
        gate_ref[h] = jax.nn.sigmoid(jnp.dot(u, maps_ref[h, :, 3 * LANES :], preferred_element_type=F32))


def lead_kernel(
    heads, dim, n_row, row_ref, own_hbm, w_hbm,
    x_ref, q_ref, k_ref, v_ref, gate_ref, maps_ref, u_ref, own_ref, w_ref, sems,
):
    row = row_ref[0]
    mine = pltpu.make_async_copy(own_hbm, own_ref, sems.at[0])
    mine.start()
    fetch = pltpu.make_async_copy(w_hbm.at[:, pl.ds(row * heads, heads)], w_ref, sems.at[1])
    fetch.start()
    clear_maps(heads, dim, maps_ref)
    mine.wait()
    split_heads(heads, dim, n_row, row, own_ref, u_ref, x_ref)
    fetch.wait()
    for m in range(w_ref.shape[0]):
        pack_map(heads, 0, m, w_ref, maps_ref)
    project(heads, u_ref, maps_ref, q_ref, k_ref, v_ref, gate_ref)


def lanes_of(block):
    rows, dim = block.shape
    return jnp.concatenate([block, jnp.zeros((rows, LANES - dim), block.dtype)], axis=1) if dim < LANES else block


def clear_maps(heads, dim, maps_ref):
    if dim < LANES:
        maps_ref[:, dim:, :] = jnp.zeros((heads, LANES - dim, maps_ref.shape[2]), BF16)


def pack_map(heads, first, m, w_ref, maps_ref):
    dim = w_ref.shape[2]
    for h in range(heads):
        maps_ref[h, :dim, m * LANES : (m + 1) * LANES] = lanes_of(w_ref[m, first + h])


def lane_blocks(sums, extra):
    blocks = sums.shape[0] // SUBLANES
    lane = lax.broadcasted_iota(jnp.int32, (SUBLANES, LANES), 1)
    tile = jnp.zeros((SUBLANES, LANES), F32)
    for b in range(blocks):
        here = lane == b
        if b < extra:
            here = jnp.logical_or(here, lane == blocks + b)
        tile = jnp.where(here, sums[b * SUBLANES : (b + 1) * SUBLANES, :], tile)
    return tile


def split_state(state):
    high = state.astype(BF16)
    low = (state - high.astype(F32)).astype(BF16)
    return jnp.concatenate([high, low], axis=0)


def attend(q, parts):
    return jnp.dot(jnp.concatenate([q, q], axis=1), parts, preferred_element_type=F32)


def finish(x, gate, attended, dim):
    inv_rms = lax.rsqrt(jnp.sum(attended * attended, axis=-1, keepdims=True) / dim + 1e-05)
    return (x + gate * attended * inv_rms).astype(BF16)


def outer_sum(k, v):
    return lax.dot_general(k, v, (((0,), (0,)), ((), ())), preferred_element_type=F32)


def stacked(first_ref, then_ref, h):
    return jnp.concatenate([first_ref[h], then_ref[h]], axis=0)


def spatial_kernel(
    heads, dim, n_row, row_ref, x_own_ref, q_own_ref, k_own_ref, v_own_ref, gate_own_ref, other_ref, maps_ref,
    mixed_ref, part_ref, u_ref, x_ref, q_ref, k_ref, v_ref, gate_ref, parts_ref,
):
    band = other_ref.shape[0]
    split_heads(heads, dim, n_row, row_ref[0], other_ref, u_ref, x_ref)
    project(heads, u_ref, maps_ref, q_ref, k_ref, v_ref, gate_ref)
    for h in range(heads):
        parts_ref[h] = split_state(outer_sum(stacked(k_own_ref, k_ref, h), stacked(v_own_ref, v_ref, h)))
    part = jnp.zeros((2 * band, LANES), F32)
    for h in range(heads):
        attended = attend(stacked(q_own_ref, q_ref, h), parts_ref[h])
        mixed = finish(stacked(x_own_ref, x_ref, h).astype(F32), stacked(gate_own_ref, gate_ref, h), attended, dim)
        mixed_ref[h] = mixed
        wide = mixed.astype(F32)
        part = part + wide * wide
    part_ref[...] = lane_blocks(jnp.sum(part, axis=-1, keepdims=True), band // SUBLANES)


def token_scale(width, blocks, part_ref, got_ref):
    total = part_ref[...] + pltpu.roll(got_ref[...], LANES - blocks // 2, 1)
    tile = lax.rsqrt(total / width + 1e-06)
    return jnp.concatenate([jnp.broadcast_to(tile[:, b : b + 1], (SUBLANES, LANES)) for b in range(blocks)], axis=0)


def early_kernel(heads, row_ref, mixed_ref, w_ref, maps_ref, k_ref, v_ref):
    clear_maps(heads, w_ref.shape[2], maps_ref)
    for m in range(w_ref.shape[0]):
        pack_map(heads, row_ref[0] * heads, m, w_ref, maps_ref)
    for h in range(heads):
        mapped = jnp.dot(mixed_ref[h], maps_ref[h, :, LANES : 3 * LANES], preferred_element_type=F32)
        k_ref[h] = jnp.maximum(mapped[:, :LANES], 0.0)
        v_ref[h] = mapped[:, LANES:].astype(BF16)


def state_kernel(heads, dim, width, k_ref, v_ref, part_ref, got_ref, state_ref, sent_ref):
    inv = token_scale(width, k_ref.shape[1] // SUBLANES, part_ref, got_ref)
    square = inv * inv
    for h in range(heads):
        state = outer_sum((k_ref[h] * square).astype(BF16), v_ref[h])
        state_ref[h] = state
        store_packed(sent_ref, h, heads, dim, state[:dim].astype(BF16))


def packing(heads, dim):
    spare = LANES - dim
    if heads > 1 and spare and dim % spare == 0:
        for left in range((dim - 1) // 16 * 16, 0, -16):
            if dim // spare * left <= (heads - 1) * dim:
                return dim - left
    return dim


def packed_rows(heads, dim):
    return (heads - 1) * dim + packing(heads, dim)


def spare_blocks(heads, dim):
    left, spare = dim - packing(heads, dim), LANES - dim
    return [(c * left, c * spare) for c in range(dim // spare)] if left else []


def store_packed(ref, h, heads, dim, block):
    at = h * dim
    if h < heads - 1:
        ref[at : at + dim, :dim] = block[:, :dim]
        return
    kept = packing(heads, dim)
    ref[at : at + kept, :] = block[:kept]
    for row, lane in spare_blocks(heads, dim):
        ref[row : row + dim - kept, dim:] = block[kept:, lane : lane + LANES - dim]


def load_packed(ref, h, heads, dim, tail_ref):
    at = h * dim
    if h < heads - 1:
        block = ref[at : at + dim, :]
    else:
        kept = packing(heads, dim)
        tail_ref[:kept, :] = ref[at : at + kept, :]
        for row, lane in spare_blocks(heads, dim):
            tail_ref[kept:dim, lane : lane + LANES - dim] = ref[row : row + dim - kept, dim:]
        block = tail_ref[:dim, :]
    lane = lax.broadcasted_iota(jnp.int32, (dim, LANES), 1)
    block = jnp.where(lane < dim, block.astype(F32), 0.0)
    if dim < LANES:
        block = jnp.concatenate([block, jnp.zeros((LANES - dim, LANES), F32)], axis=0)
    return block


def write_out(heads, dim, n_row, row, mixed_ref, gate_ref, attended_ref, scaled_ref, out_hbm, out_ref, sems):
    band = mixed_ref.shape[1] // n_row
    for h in range(heads):
        attended = attended_ref[h]
        scaled_ref[h] = attended * lax.rsqrt(jnp.sum(attended * attended, axis=-1, keepdims=True) / dim + 1e-05)
    copies = []
    for b, place in enumerate((row, n_row - 1 - row)):
        at = slice(b * band, (b + 1) * band)
        for h in range(heads):
            new = (mixed_ref[h, at, :].astype(F32) + gate_ref[h, at, :] * scaled_ref[h, at, :]).astype(BF16)
            out_ref[at, h * dim : (h + 1) * dim] = new[:, :dim]
        to = pl.ds(pl.multiple_of(place * band, band), band)
        copies.append(pltpu.make_async_copy(out_ref.at[at], out_hbm.at[to], sems.at[b]))
        copies[-1].start()
    for copy in copies:
        copy.wait()


def query_kernel(
    heads, dim, width, n_row, taken, row_ref, place_ref, mixed_ref, part_ref, got_part_ref, maps_ref, state_ref, *refs
):
    got_refs, (q_ref, gate_ref, base_ref, out_hbm, out_ref, scaled_ref, sum_ref, tail_ref, sems) = refs[:-9], refs[-9:]
    place = place_ref[0]
    earlier = jnp.zeros(sum_ref.shape, F32)
    for turn, got_ref in enumerate(got_refs):
        earlier = earlier + jnp.where(taken(place, turn), got_ref[...].astype(F32), 0.0)
    sum_ref[...] = earlier
    inv = token_scale(width, mixed_ref.shape[1] // SUBLANES, part_ref, got_part_ref)
    for h in range(heads):
        u = (mixed_ref[h].astype(F32) * inv).astype(BF16)
        q = jnp.maximum(jnp.dot(u, maps_ref[h, :, :LANES], preferred_element_type=F32), 0.0).astype(BF16)
        q_ref[h] = q
        gate_ref[h] = jax.nn.sigmoid(jnp.dot(u, maps_ref[h, :, 3 * LANES :], preferred_element_type=F32))
    for h in range(heads):
        state = state_ref[h]
        if got_refs:
            state = state + load_packed(sum_ref, h, heads, dim, tail_ref)
        base_ref[h] = attend(q_ref[h], split_state(state))
    write_out(heads, dim, n_row, row_ref[0], mixed_ref, gate_ref, base_ref, scaled_ref, out_hbm, out_ref, sems)


def finish_kernel(
    heads, dim, n_row, taken, turn, row_ref, place_ref, mixed_ref, q_ref, gate_ref, base_ref, got_ref, first_hbm,
    out_hbm, out_ref, state_ref, tail_ref, attended_ref, sems,
):
    @pl.when(taken(place_ref[0], turn))
    def _():
        for h in range(heads):
            state_ref[h] = load_packed(got_ref, h, heads, dim, tail_ref).astype(BF16)
        for h in range(heads):
            attended_ref[h] = base_ref[h] + jnp.dot(q_ref[h], state_ref[h], preferred_element_type=F32)
        write_out(
            heads, dim, n_row, row_ref[0], mixed_ref, gate_ref, attended_ref, attended_ref, out_hbm, out_ref, sems
        )


def exchange_rounds(sent, axis):
    size = lax.axis_size(axis)
    if size & (size - 1):
        raise ValueError("unsupported mesh")
    got, masks = [], []
    total = sent.astype(F32)
    block = 1
    while block < size:
        if 4 * block <= size:
            turn = [3 * block, 2 * block, block]
        else:
            turn = [block + block // 2]
        arrived = [lax.ppermute(sent, axis, [(i, i ^ mask) for i in range(size)]) for mask in turn]
        got += arrived
        masks += turn
        block *= len(turn) + 1
        if block < size:
            for one in arrived:
                total = total + one.astype(F32)
            sent = total.astype(BF16)

    def taken(place, turn):
        return (place >> (masks[turn].bit_length() - 1)) & 1 == 1

    return got, taken


def body(latents, spatial_weights, causal_weights):
    frames, rows, cols, width = latents.shape
    maps, all_heads, dim, _ = spatial_weights.shape
    n_row = lax.axis_size("row")
    if frames != 1 or n_row != 2 or dim > LANES or 3 * rows * cols > SUBLANES * LANES or lax.axis_size("frame") < 2:
        raise ValueError("unsupported shapes")
    heads = all_heads // n_row
    band = rows * cols
    tokens = n_row * band
    row = jnp.reshape(lax.axis_index("row"), (1,)).astype(jnp.int32)
    place = jnp.reshape(lax.axis_index("frame"), (1,)).astype(jnp.int32)
    swap = [(i, n_row - 1 - i) for i in range(n_row)]

    def shape(*dims, kind=BF16):
        return jax.ShapeDtypeStruct(dims, kind)

    packed_maps = shape(heads, LANES, maps * LANES)
    fetched = pltpu.VMEM((maps, heads, dim, dim), BF16)
    band_head = pltpu.VMEM((heads, band, LANES), BF16)
    band_gates = pltpu.VMEM((heads, band, LANES), F32)
    gates = pltpu.VMEM((heads, tokens, LANES), F32)
    own_outs = [shape(heads, band, LANES)] * 4 + [shape(heads, band, LANES, kind=F32)]
    head_flops = 2 * tokens * heads * LANES * LANES

    own = latents.reshape(band, width)
    own_hbm = pltpu.with_memory_space_constraint(own, pltpu.HBM)
    spatial_weights = pltpu.with_memory_space_constraint(spatial_weights, pltpu.HBM)
    other = lax.ppermute(own, "row", swap)
    *of_own, maps_s = call(
        functools.partial(lead_kernel, heads, dim, n_row), "lead", own_outs + [packed_maps],
        [row, own_hbm, spatial_weights], [SMEM, HBM, HBM],
        [band_head, pltpu.VMEM((band, width), BF16), fetched, pltpu.SemaphoreType.DMA((2,))],
        flops=head_flops * 2,
    )
    mixed, part = call(
        functools.partial(spatial_kernel, heads, dim, n_row), "spatial",
        [shape(heads, tokens, LANES), shape(SUBLANES, LANES, kind=F32)],
        [row, *of_own, other, maps_s], [SMEM] + [VMEM] * 7,
        [band_head] * 5 + [band_gates, pltpu.VMEM((heads, 2 * LANES, LANES), BF16)],
        flops=head_flops * 4,
    )
    got_part = lax.ppermute(part, "row", swap)
    maps_c, k, v = call(
        functools.partial(early_kernel, heads), "early",
        [packed_maps, shape(heads, tokens, LANES, kind=F32), shape(heads, tokens, LANES)],
        [row, mixed, causal_weights], [SMEM, VMEM, VMEM], flops=head_flops * 2,
    )
    state, sent = call(
        functools.partial(state_kernel, heads, dim, width), "state",
        [shape(heads, LANES, LANES, kind=F32), shape(packed_rows(heads, dim), LANES)],
        [k, v, part, got_part], [VMEM] * 4, flops=head_flops,
    )
    got, taken = exchange_rounds(sent, "frame")
    packed_sum = pltpu.VMEM((packed_rows(heads, dim), LANES), F32)
    whole = shape(tokens, heads * dim)
    writing = [pltpu.VMEM((tokens, heads * dim), BF16)]
    done = [pltpu.SemaphoreType.DMA((n_row,))]
    q, gate, base, out = call(
        functools.partial(query_kernel, heads, dim, width, n_row, taken), "query",
        [shape(heads, tokens, LANES), shape(heads, tokens, LANES, kind=F32), shape(heads, tokens, LANES, kind=F32), whole],
        [row, place, mixed, part, got_part, maps_c, state, *got[:-1]], [SMEM] * 2 + [VMEM] * (4 + len(got)),
        writing + [gates, packed_sum, pltpu.VMEM((LANES, LANES), F32)] + done,
        flops=head_flops * 4, out_specs=[VMEM] * 3 + [HBM],
    )
    (out,) = call(
        functools.partial(finish_kernel, heads, dim, n_row, taken, len(got) - 1), "finish", [whole],
        [row, place, mixed, q, gate, base, got[-1], out], [SMEM] * 2 + [VMEM] * 5 + [HBM],
        writing + [pltpu.VMEM((heads, LANES, LANES), BF16), pltpu.VMEM((LANES, LANES), BF16), gates] + done,
        flops=head_flops, out_specs=[HBM], aliases={7: 0},
    )
    return out.reshape(frames, n_row * rows, cols, heads * dim)


def solution(mesh):
    in_specs = (P(("group", "frame"), "row", None, None), P(), P())
    out_specs = P(("group", "frame"), None, None, "row")
    return jax.shard_map(body, mesh=mesh, in_specs=in_specs, out_specs=out_specs, check_vma=False)
```

```python
import functools

import jax
import jax.numpy as jnp
from jax import lax
from jax.experimental import pallas as pl
from jax.experimental.pallas import tpu as pltpu
from jax.sharding import PartitionSpec as P

LANES = 128
SUBLANES = 8
F32 = jnp.float32
BF16 = jnp.bfloat16
VMEM = pl.BlockSpec(memory_space=pltpu.VMEM)
SMEM = pl.BlockSpec(memory_space=pltpu.SMEM)
HBM = pl.BlockSpec(memory_space=pltpu.HBM)


def call(kernel, name, outs, operands, in_specs, scratch=(), flops=0, limit=16 << 20, out_specs=None, aliases=None):
    n_bytes = sum(o.size * o.dtype.itemsize for o in operands)
    n_bytes += sum(o.size * o.dtype.itemsize for o in outs)
    return pl.pallas_call(
        kernel,
        name=name,
        out_shape=tuple(outs),
        in_specs=in_specs,
        out_specs=tuple(out_specs or [VMEM for _ in outs]),
        scratch_shapes=list(scratch),
        input_output_aliases=aliases or {},
        compiler_params=pltpu.CompilerParams(vmem_limit_bytes=limit),
        cost_estimate=pl.CostEstimate(flops=flops, bytes_accessed=n_bytes, transcendentals=0),
    )(*operands)


def split_heads(heads, dim, n_row, row, src_ref, u_ref, x_ref):
    band, width = src_ref.shape
    full = src_ref[...].astype(F32)
    inv = lax.rsqrt(jnp.sum(full * full, axis=-1, keepdims=True) / width + 1e-06)
    inv = jnp.broadcast_to(inv, (band, LANES))
    for r in range(n_row):

        @pl.when(row == r)
        def _():
            for h in range(heads):
                lo = (r * heads + h) * dim
                x_ref[h] = lanes_of(src_ref[:, lo : lo + dim])

    for h in range(heads):
        u_ref[h] = (x_ref[h].astype(F32) * inv).astype(BF16)


def project(heads, u_ref, maps_ref, q_ref, k_ref, v_ref, gate_ref):
    for h in range(heads):
        mapped = jnp.dot(u_ref[h], maps_ref[h, :, LANES : 3 * LANES], preferred_element_type=F32)
        k_ref[h] = jnp.maximum(mapped[:, :LANES], 0.0).astype(BF16)
        v_ref[h] = mapped[:, LANES:].astype(BF16)
    for h in range(heads):
        u = u_ref[h]
        q_ref[h] = jnp.maximum(jnp.dot(u, maps_ref[h, :, :LANES], preferred_element_type=F32), 0.0).astype(BF16)
        gate_ref[h] = jax.nn.sigmoid(jnp.dot(u, maps_ref[h, :, 3 * LANES :], preferred_element_type=F32))


def lead_kernel(
    heads, dim, n_row, row_ref, own_hbm, w_hbm,
    x_ref, q_ref, k_ref, v_ref, gate_ref, maps_ref, u_ref, own_ref, w_ref, sems,
):
    row = row_ref[0]
    mine = pltpu.make_async_copy(own_hbm, own_ref, sems.at[0])
    mine.start()
    fetch = pltpu.make_async_copy(w_hbm.at[:, pl.ds(row * heads, heads)], w_ref, sems.at[1])
    fetch.start()
    clear_maps(heads, dim, maps_ref)
    mine.wait()
    split_heads(heads, dim, n_row, row, own_ref, u_ref, x_ref)
    fetch.wait()
    for m in range(w_ref.shape[0]):
        pack_map(heads, 0, m, w_ref, maps_ref)
    project(heads, u_ref, maps_ref, q_ref, k_ref, v_ref, gate_ref)


def lanes_of(block):
    rows, dim = block.shape
    return jnp.concatenate([block, jnp.zeros((rows, LANES - dim), block.dtype)], axis=1) if dim < LANES else block


def clear_maps(heads, dim, maps_ref):
    if dim < LANES:
        maps_ref[:, dim:, :] = jnp.zeros((heads, LANES - dim, maps_ref.shape[2]), BF16)


def pack_map(heads, first, m, w_ref, maps_ref):
    dim = w_ref.shape[2]
    for h in range(heads):
        maps_ref[h, :dim, m * LANES : (m + 1) * LANES] = lanes_of(w_ref[m, first + h])


def lane_blocks(sums, extra):
    blocks = sums.shape[0] // SUBLANES
    lane = lax.broadcasted_iota(jnp.int32, (SUBLANES, LANES), 1)
    tile = jnp.zeros((SUBLANES, LANES), F32)
    for b in range(blocks):
        here = lane == b
        if b < extra:
            here = jnp.logical_or(here, lane == blocks + b)
        tile = jnp.where(here, sums[b * SUBLANES : (b + 1) * SUBLANES, :], tile)
    return tile


def split_state(state):
    high = state.astype(BF16)
    low = (state - high.astype(F32)).astype(BF16)
    return jnp.concatenate([high, low], axis=0)


def attend(q, parts):
    return jnp.dot(jnp.concatenate([q, q], axis=1), parts, preferred_element_type=F32)


def finish(x, gate, attended, dim):
    inv_rms = lax.rsqrt(jnp.sum(attended * attended, axis=-1, keepdims=True) / dim + 1e-05)
    return (x + gate * attended * inv_rms).astype(BF16)


def outer_sum(k, v):
    return lax.dot_general(k, v, (((0,), (0,)), ((), ())), preferred_element_type=F32)


def stacked(first_ref, then_ref, h):
    return jnp.concatenate([first_ref[h], then_ref[h]], axis=0)


def spatial_kernel(
    heads, dim, n_row, row_ref, x_own_ref, q_own_ref, k_own_ref, v_own_ref, gate_own_ref, other_ref, maps_ref,
    mixed_ref, part_ref, u_ref, x_ref, q_ref, k_ref, v_ref, gate_ref, parts_ref,
):
    band = other_ref.shape[0]
    split_heads(heads, dim, n_row, row_ref[0], other_ref, u_ref, x_ref)
    project(heads, u_ref, maps_ref, q_ref, k_ref, v_ref, gate_ref)
    for h in range(heads):
        parts_ref[h] = split_state(outer_sum(stacked(k_own_ref, k_ref, h), stacked(v_own_ref, v_ref, h)))
    part = jnp.zeros((2 * band, LANES), F32)
    for h in range(heads):
        attended = attend(stacked(q_own_ref, q_ref, h), parts_ref[h])
        mixed = finish(stacked(x_own_ref, x_ref, h).astype(F32), stacked(gate_own_ref, gate_ref, h), attended, dim)
        mixed_ref[h] = mixed
        wide = mixed.astype(F32)
        part = part + wide * wide
    part_ref[...] = lane_blocks(jnp.sum(part, axis=-1, keepdims=True), band // SUBLANES)


def token_scale(width, blocks, part_ref, got_ref):
    total = part_ref[...] + pltpu.roll(got_ref[...], LANES - blocks // 2, 1)
    tile = lax.rsqrt(total / width + 1e-06)
    return jnp.concatenate([jnp.broadcast_to(tile[:, b : b + 1], (SUBLANES, LANES)) for b in range(blocks)], axis=0)


def early_kernel(heads, row_ref, mixed_ref, w_ref, maps_ref, k_ref, v_ref):
    clear_maps(heads, w_ref.shape[2], maps_ref)
    for m in range(w_ref.shape[0]):
        pack_map(heads, row_ref[0] * heads, m, w_ref, maps_ref)
    for h in range(heads):
        mapped = jnp.dot(mixed_ref[h], maps_ref[h, :, LANES : 3 * LANES], preferred_element_type=F32)
        k_ref[h] = jnp.maximum(mapped[:, :LANES], 0.0).astype(BF16).T
        v_ref[h] = mapped[:, LANES:]


def state_kernel(heads, dim, width, k_ref, v_ref, part_ref, got_ref, state_ref, sent_ref):
    inv = token_scale(width, v_ref.shape[1] // SUBLANES, part_ref, got_ref)
    square = inv * inv
    for h in range(heads):
        state = jnp.dot(k_ref[h], (v_ref[h] * square).astype(BF16), preferred_element_type=F32)
        state_ref[h] = state
        store_packed(sent_ref, h, heads, dim, state[:dim].astype(BF16))


def packing(heads, dim):
    spare = LANES - dim
    if heads > 1 and spare and dim % spare == 0:
        for left in range((dim - 1) // 16 * 16, 0, -16):
            if dim // spare * left <= (heads - 1) * dim:
                return dim - left
    return dim


def packed_rows(heads, dim):
    return (heads - 1) * dim + packing(heads, dim)


def spare_blocks(heads, dim):
    left, spare = dim - packing(heads, dim), LANES - dim
    return [(c * left, c * spare) for c in range(dim // spare)] if left else []


def store_packed(ref, h, heads, dim, block):
    at = h * dim
    if h < heads - 1:
        ref[at : at + dim, :dim] = block[:, :dim]
        return
    kept = packing(heads, dim)
    ref[at : at + kept, :] = block[:kept]
    for row, lane in spare_blocks(heads, dim):
        ref[row : row + dim - kept, dim:] = block[kept:, lane : lane + LANES - dim]


def load_packed(ref, h, heads, dim, tail_ref):
    at = h * dim
    if h < heads - 1:
        block = ref[at : at + dim, :]
    else:
        kept = packing(heads, dim)
        tail_ref[:kept, :] = ref[at : at + kept, :]
        for row, lane in spare_blocks(heads, dim):
            tail_ref[kept:dim, lane : lane + LANES - dim] = ref[row : row + dim - kept, dim:]
        block = tail_ref[:dim, :]
    lane = lax.broadcasted_iota(jnp.int32, (dim, LANES), 1)
    block = jnp.where(lane < dim, block.astype(F32), 0.0)
    if dim < LANES:
        block = jnp.concatenate([block, jnp.zeros((LANES - dim, LANES), F32)], axis=0)
    return block


def write_out(heads, dim, n_row, row, mixed_ref, gate_ref, attended_ref, scaled_ref, out_hbm, out_ref, sems):
    band = mixed_ref.shape[1] // n_row
    for h in range(heads):
        attended = attended_ref[h]
        scaled_ref[h] = attended * lax.rsqrt(jnp.sum(attended * attended, axis=-1, keepdims=True) / dim + 1e-05)
    copies = []
    for b, place in enumerate((row, n_row - 1 - row)):
        at = slice(b * band, (b + 1) * band)
        for h in range(heads):
            new = (mixed_ref[h, at, :].astype(F32) + gate_ref[h, at, :] * scaled_ref[h, at, :]).astype(BF16)
            out_ref[at, h * dim : (h + 1) * dim] = new[:, :dim]
        to = pl.ds(pl.multiple_of(place * band, band), band)
        copies.append(pltpu.make_async_copy(out_ref.at[at], out_hbm.at[to], sems.at[b]))
        copies[-1].start()
    for copy in copies:
        copy.wait()


def query_kernel(
    heads, dim, width, n_row, taken, row_ref, place_ref, mixed_ref, part_ref, got_part_ref, maps_ref, state_ref, *refs
):
    got_refs, (q_ref, gate_ref, base_ref, out_hbm, out_ref, scaled_ref, sum_ref, tail_ref, sems) = refs[:-9], refs[-9:]
    place = place_ref[0]
    earlier = jnp.zeros(sum_ref.shape, F32)
    for turn, got_ref in enumerate(got_refs):
        earlier = earlier + jnp.where(taken(place, turn), got_ref[...].astype(F32), 0.0)
    sum_ref[...] = earlier
    inv = token_scale(width, mixed_ref.shape[1] // SUBLANES, part_ref, got_part_ref)
    for h in range(heads):
        u = (mixed_ref[h].astype(F32) * inv).astype(BF16)
        q = jnp.maximum(jnp.dot(u, maps_ref[h, :, :LANES], preferred_element_type=F32), 0.0).astype(BF16)
        q_ref[h] = q
        gate_ref[h] = jax.nn.sigmoid(jnp.dot(u, maps_ref[h, :, 3 * LANES :], preferred_element_type=F32))
    for h in range(heads):
        state = state_ref[h]
        if got_refs:
            state = state + load_packed(sum_ref, h, heads, dim, tail_ref)
        base_ref[h] = attend(q_ref[h], split_state(state))
    write_out(heads, dim, n_row, row_ref[0], mixed_ref, gate_ref, base_ref, scaled_ref, out_hbm, out_ref, sems)


def finish_kernel(
    heads, dim, n_row, taken, turn, row_ref, place_ref, mixed_ref, q_ref, gate_ref, base_ref, got_ref, first_hbm,
    out_hbm, out_ref, state_ref, tail_ref, attended_ref, sems,
):
    @pl.when(taken(place_ref[0], turn))
    def _():
        for h in range(heads):
            state_ref[h] = load_packed(got_ref, h, heads, dim, tail_ref).astype(BF16)
        for h in range(heads):
            attended_ref[h] = base_ref[h] + jnp.dot(q_ref[h], state_ref[h], preferred_element_type=F32)
        write_out(
            heads, dim, n_row, row_ref[0], mixed_ref, gate_ref, attended_ref, attended_ref, out_hbm, out_ref, sems
        )


def exchange_rounds(sent, axis):
    size = lax.axis_size(axis)
    if size & (size - 1):
        raise ValueError("unsupported mesh")
    got, masks = [], []
    total = sent.astype(F32)
    block = 1
    while block < size:
        if 4 * block <= size:
            turn = [3 * block, 2 * block, block]
        else:
            turn = [block + block // 2]
        arrived = [lax.ppermute(sent, axis, [(i, i ^ mask) for i in range(size)]) for mask in turn]
        got += arrived
        masks += turn
        block *= len(turn) + 1
        if block < size:
            for one in arrived:
                total = total + one.astype(F32)
            sent = total.astype(BF16)

    def taken(place, turn):
        return (place >> (masks[turn].bit_length() - 1)) & 1 == 1

    return got, taken


def body(latents, spatial_weights, causal_weights):
    frames, rows, cols, width = latents.shape
    maps, all_heads, dim, _ = spatial_weights.shape
    n_row = lax.axis_size("row")
    if frames != 1 or n_row != 2 or dim > LANES or 3 * rows * cols > SUBLANES * LANES or lax.axis_size("frame") < 2:
        raise ValueError("unsupported shapes")
    heads = all_heads // n_row
    band = rows * cols
    tokens = n_row * band
    row = jnp.reshape(lax.axis_index("row"), (1,)).astype(jnp.int32)
    place = jnp.reshape(lax.axis_index("frame"), (1,)).astype(jnp.int32)
    swap = [(i, n_row - 1 - i) for i in range(n_row)]

    def shape(*dims, kind=BF16):
        return jax.ShapeDtypeStruct(dims, kind)

    packed_maps = shape(heads, LANES, maps * LANES)
    fetched = pltpu.VMEM((maps, heads, dim, dim), BF16)
    band_head = pltpu.VMEM((heads, band, LANES), BF16)
    band_gates = pltpu.VMEM((heads, band, LANES), F32)
    gates = pltpu.VMEM((heads, tokens, LANES), F32)
    own_outs = [shape(heads, band, LANES)] * 4 + [shape(heads, band, LANES, kind=F32)]
    head_flops = 2 * tokens * heads * LANES * LANES

    own = latents.reshape(band, width)
    own_hbm = pltpu.with_memory_space_constraint(own, pltpu.HBM)
    spatial_weights = pltpu.with_memory_space_constraint(spatial_weights, pltpu.HBM)
    other = lax.ppermute(own, "row", swap)
    *of_own, maps_s = call(
        functools.partial(lead_kernel, heads, dim, n_row), "lead", own_outs + [packed_maps],
        [row, own_hbm, spatial_weights], [SMEM, HBM, HBM],
        [band_head, pltpu.VMEM((band, width), BF16), fetched, pltpu.SemaphoreType.DMA((2,))],
        flops=head_flops * 2,
    )
    mixed, part = call(
        functools.partial(spatial_kernel, heads, dim, n_row), "spatial",
        [shape(heads, tokens, LANES), shape(SUBLANES, LANES, kind=F32)],
        [row, *of_own, other, maps_s], [SMEM] + [VMEM] * 7,
        [band_head] * 5 + [band_gates, pltpu.VMEM((heads, 2 * LANES, LANES), BF16)],
        flops=head_flops * 4,
    )
    got_part = lax.ppermute(part, "row", swap)
    maps_c, k, v = call(
        functools.partial(early_kernel, heads), "early",
        [packed_maps, shape(heads, LANES, tokens), shape(heads, tokens, LANES, kind=F32)],
        [row, mixed, causal_weights], [SMEM, VMEM, VMEM], flops=head_flops * 2,
    )
    state, sent = call(
        functools.partial(state_kernel, heads, dim, width), "state",
        [shape(heads, LANES, LANES, kind=F32), shape(packed_rows(heads, dim), LANES)],
        [k, v, part, got_part], [VMEM] * 4, flops=head_flops,
    )
    got, taken = exchange_rounds(sent, "frame")
    packed_sum = pltpu.VMEM((packed_rows(heads, dim), LANES), F32)
    whole = shape(tokens, heads * dim)
    writing = [pltpu.VMEM((tokens, heads * dim), BF16)]
    done = [pltpu.SemaphoreType.DMA((n_row,))]
    q, gate, base, out = call(
        functools.partial(query_kernel, heads, dim, width, n_row, taken), "query",
        [shape(heads, tokens, LANES), shape(heads, tokens, LANES, kind=F32), shape(heads, tokens, LANES, kind=F32), whole],
        [row, place, mixed, part, got_part, maps_c, state, *got[:-1]], [SMEM] * 2 + [VMEM] * (4 + len(got)),
        writing + [gates, packed_sum, pltpu.VMEM((LANES, LANES), F32)] + done,
        flops=head_flops * 4, out_specs=[VMEM] * 3 + [HBM],
    )
    (out,) = call(
        functools.partial(finish_kernel, heads, dim, n_row, taken, len(got) - 1), "finish", [whole],
        [row, place, mixed, q, gate, base, got[-1], out], [SMEM] * 2 + [VMEM] * 5 + [HBM],
        writing + [pltpu.VMEM((heads, LANES, LANES), BF16), pltpu.VMEM((LANES, LANES), BF16), gates] + done,
        flops=head_flops, out_specs=[HBM], aliases={7: 0},
    )
    return out.reshape(frames, n_row * rows, cols, heads * dim)


def solution(mesh):
    in_specs = (P(("group", "frame"), "row", None, None), P(), P())
    out_specs = P(("group", "frame"), None, None, "row")
    return jax.shard_map(body, mesh=mesh, in_specs=in_specs, out_specs=out_specs, check_vma=False)
```
